128 devices in a mesh: ctx: 16 (over x, y), head: 2 (over core), dp: 4 (over z).
Axes of the slice: x: 4, y: 4, z: 4, core: 2. Of those that a mesh axis runs over, the one named last changes fastest.
Arguments:
- query_matrix: bfloat16 [16384, 4096], P(('dp', 'ctx'), 'head'), parts along dimension 0
- key_matrix: bfloat16 [16384, 512], P(('dp', 'ctx'), 'head'), parts along dimension 0
- value_matrix: bfloat16 [16384, 512], P(('dp', 'ctx'), 'head'), parts along dimension 0, may hold values from -6 to 6
- output_cotangent: bfloat16 [16384, 4096], P(('dp', 'ctx'), 'head'), parts along dimension 0, may hold values from -6 to 6
- doc_lengths: int32 [32], P('dp'), parts along dimension 0, may hold values from 1 to 2304, 4096 in all
- block_dest: int32 [1024], P('dp'), parts along dimension 0, may hold values from 0 to 255, as said below
Outputs:
- attention_result: bfloat16 [16384, 4096], P(('dp', 'ctx'), 'head'), parts along dimension 0
- query_gradient: bfloat16 [16384, 4096], P(('dp', 'ctx'), 'head'), parts along dimension 0
- key_gradient: bfloat16 [16384, 512], P(('dp', 'ctx'), 'head'), parts along dimension 0
- value_gradient: bfloat16 [16384, 512], P(('dp', 'ctx'), 'head'), parts along dimension 0
The draws below stay inside these ranges and needn't reach their ends.
There are 4 independent parts, one for each index of `dp`. The reference program is written for one: setup_inputs(seed, part) draws one part's arguments, and reference() takes and returns one part's arrays. A program takes and returns all parts, laid end to end along the dimension named above; each array names one. Nothing has to cross between parts.
Inputs may be any that keep to these rules, and one draw needn't show every extreme that they name: `doc_lengths`: the 8 lengths sum to 4096. `block_dest`: a permutation; the 16 blocks that start on one index of ctx go at most 2 to one index of ctx (slot k lies on index k // 16), and exactly 2 for some pair of indices.
All inputs are finite; a program needn't handle non-finite values.
Results may differ from the reference program's by a relative error of at most 0.03.
Values may be sent and summed in bfloat16 or wider, within the bound.
A program may use at most 128 MiB of HBM per device.

```python
import math
import jax
import jax.numpy as jnp
import numpy as np
from jax import lax

QUERY_HEADS = 32
KEY_VALUE_HEADS = 4
HEAD_SIZE = 128
TOKENS_PER_SHARD = 256
BLK = 16
NDOCS = 8
PACKED_TOKENS = 4096
BPD = 16
NBLK = 256
CAP = 2
N_CTX = 16


def common_keys(key):
    return jax.random.normal(jax.random.fold_in(key, 11), (PACKED_TOKENS, KEY_VALUE_HEADS * HEAD_SIZE), jnp.float32)


def draw_key_matrix(key, part):
    return common_keys(key).astype(jnp.bfloat16)


def draw_query_matrix(key, part):
    base = jax.random.normal(jax.random.fold_in(key, 12), (PACKED_TOKENS, QUERY_HEADS * HEAD_SIZE), jnp.float32)
    return base.astype(jnp.bfloat16)


def forced_column(column_key, source_fixed, half_step):
    devices_row = jnp.arange(N_CTX, dtype=jnp.int32)
    perm = jax.random.permutation(column_key, devices_row).astype(jnp.int32)
    wanted = ((source_fixed + half_step) % N_CTX).astype(jnp.int32)
    holder = jnp.sum(jnp.where(perm == wanted, devices_row, 0)).astype(jnp.int32)
    fixed_value = jnp.sum(jnp.where(devices_row == source_fixed, perm, 0)).astype(jnp.int32)
    swapped = jnp.where(devices_row == holder, fixed_value, perm)
    return jnp.where(devices_row == source_fixed, wanted, swapped).astype(jnp.int32)


def draw_block_dest(key, part):
    key_others, key_order, key_slots, key_source, key_columns = jax.random.split(key, 5)
    half_step = N_CTX // 2
    sources = jnp.arange(N_CTX, dtype=jnp.int32)[:, None]
    if BPD == CAP:
        source_fixed = jax.random.randint(key_source, (), 0, N_CTX).astype(jnp.int32)
        column_keys = jax.random.split(key_columns, BPD)
        columns = jnp.stack([forced_column(column_keys[index], source_fixed, half_step) for index in range(BPD)])
        target = jnp.transpose(columns)
    else:
        others = (half_step + 1 + jnp.arange((N_CTX - 1) * CAP) // CAP) % N_CTX
        others = jax.random.permutation(key_others, others)
        offsets = jnp.concatenate([jnp.full((CAP,), half_step), others[:BPD - CAP]])
        offsets = jax.random.permutation(key_order, offsets)
        target = (sources + offsets[None, :]) % N_CTX
    slot_keys = jax.random.split(key_slots, N_CTX)
    slot_table = jnp.stack([jax.random.permutation(slot_keys[index], jnp.arange(BPD)) for index in range(N_CTX)]).astype(jnp.int32)
    columns_index = jnp.arange(BPD, dtype=jnp.int32)[None, :]
    slot_value = slot_table[target, jnp.broadcast_to(columns_index, target.shape)]
    return (target * BPD + slot_value).reshape(NBLK).astype(jnp.int32)


def block_levels(key, shape, cuts, smallest, high):
    level = 1.0
    for position, shards_of in cuts:
        draws = jax.random.uniform(jax.random.fold_in(jax.random.fold_in(key, 6), position), (shards_of,), jnp.float32, smallest / len(cuts), high / len(cuts))
        level = level * jnp.repeat(jnp.exp(draws), shape[position] // shards_of).reshape((-1,) + (1,) * (len(shape) - 1 - position))
    return level


def length_profile(number_of, total, reach, slope):
    loads = [(1 << 20) // math.isqrt(standing ** slope) + 1 for standing in range(2, number_of + 1)]
    surplus, holding = total - reach - (number_of - 1), [1] * (number_of - 1)
    while surplus > 0:
        candidates = [i for i in range(number_of - 1) if holding[i] < reach]
        mass, left = sum([loads[i] for i in candidates]), surplus
        for i in candidates:
            addition = min(reach - holding[i], max(1, left * loads[i] // mass), surplus)
            holding[i] = holding[i] + addition
            surplus = surplus - addition
    return np.array([reach] + holding)


def ragged(own_key, count, total, limit, skew):
    if count == 2:
        one = jax.random.randint(own_key, (), max(1, total - limit), min(limit, total - 1) + 1)
        return jnp.stack([one, total - one])
    sizes = jnp.asarray(length_profile(count, total, limit, skew), jnp.int32)
    couples = (count - 1) // 2
    donor, receiver = sizes[1:1 + 2 * couples:2], sizes[2:2 + 2 * couples:2]
    margin = jnp.minimum(donor - 1, limit - receiver)
    shifted = jax.random.randint(jax.random.fold_in(own_key, 1), (couples,), 0, 1 << 20) % (margin + 1)
    sizes = sizes.at[1:1 + 2 * couples:2].set(donor - shifted).at[2:2 + 2 * couples:2].set(receiver + shifted)
    return sizes[jax.random.permutation(jax.random.fold_in(own_key, 2), count)]


def noise(rng, shape, spread, reach, cuts=(), kind=jnp.bfloat16):
    array = spread * jax.random.normal(rng, shape, jnp.float32)
    if cuts:
        array = array * block_levels(rng, shape, cuts, -0.22, 0.18)
    return jnp.clip(array, -reach, reach).astype(kind)


def setup_inputs(seed: int = 0, part: int = 0) -> dict:
    key_list = jax.random.split(jax.random.key(seed), 7)
    part_keys = jax.random.split(jax.random.fold_in(key_list[6], part), 7)
    query_matrix = draw_query_matrix(jax.random.fold_in(jax.random.fold_in(key_list[6], part), 71), part)
    key_matrix = draw_key_matrix(jax.random.fold_in(jax.random.fold_in(key_list[6], part), 71), part)
    value_matrix = noise(part_keys[2], (PACKED_TOKENS, KEY_VALUE_HEADS * HEAD_SIZE), 1.0, 6.0, ((0, 16), (1, 2)))
    output_cotangent = noise(part_keys[3], (PACKED_TOKENS, QUERY_HEADS * HEAD_SIZE), 1.0, 6.0, ((0, 16), (1, 2)))
    doc_lengths = ragged(part_keys[4], NDOCS, PACKED_TOKENS, PACKED_TOKENS // 2 + TOKENS_PER_SHARD, 2).astype(jnp.int32)
    block_dest = draw_block_dest(jax.random.fold_in(jax.random.fold_in(key_list[6], part), 71), part)
    return {"query_matrix": query_matrix, "key_matrix": key_matrix, "value_matrix": value_matrix, "output_cotangent": output_cotangent, "doc_lengths": doc_lengths, "block_dest": block_dest}


def doc_starts(doc_lengths, positions):
    doc_ends = jnp.cumsum(doc_lengths).astype(jnp.int32)
    chosen = jnp.where(doc_ends[None, :] <= positions[:, None], doc_lengths[None, :], 0)
    return lax.optimization_barrier(jnp.sum(chosen, axis=1)).astype(jnp.int32)

def reference(query_matrix, key_matrix, value_matrix, output_cotangent, doc_lengths, block_dest):
    head_group = QUERY_HEADS // KEY_VALUE_HEADS
    scaling = 1.0 / math.sqrt(HEAD_SIZE)
    window = min(PACKED_TOKENS, PACKED_TOKENS // 2 + 2 * TOKENS_PER_SHARD)
    gathered_keys = key_matrix.astype(jnp.float32).reshape(PACKED_TOKENS, KEY_VALUE_HEADS, HEAD_SIZE)
    gathered_values = value_matrix.astype(jnp.float32).reshape(PACKED_TOKENS, KEY_VALUE_HEADS, HEAD_SIZE)

    def block_step(carry, index):
        key_gradient, value_gradient = carry
        leading_row = (index * TOKENS_PER_SHARD).astype(jnp.int32)
        key_first = jnp.clip(leading_row + TOKENS_PER_SHARD - window, 0, PACKED_TOKENS - window).astype(jnp.int32)
        key_block = lax.dynamic_slice_in_dim(gathered_keys, key_first, window, 0)
        value_block = lax.dynamic_slice_in_dim(gathered_values, key_first, window, 0)
        key_pos = key_first + jnp.arange(window, dtype=jnp.int32)
        current_query_block = lax.dynamic_slice_in_dim(query_matrix, leading_row, TOKENS_PER_SHARD, 0).astype(jnp.float32).reshape(TOKENS_PER_SHARD, KEY_VALUE_HEADS, head_group, HEAD_SIZE)
        block_gradient = lax.dynamic_slice_in_dim(output_cotangent, leading_row, TOKENS_PER_SHARD, 0).astype(jnp.float32).reshape(TOKENS_PER_SHARD, KEY_VALUE_HEADS, head_group, HEAD_SIZE)
        query_pos = leading_row + jnp.arange(TOKENS_PER_SHARD, dtype=jnp.int32)
        starts = doc_starts(doc_lengths, query_pos)
        visible = (key_pos[None, :] >= starts[:, None]) & (key_pos[None, :] <= query_pos[:, None])
        scores = jnp.einsum('rgjd,kgd->gjrk', current_query_block, key_block) * scaling
        scores = jnp.where(visible, scores, -jnp.inf)
        peak = lax.optimization_barrier(jnp.max(scores, axis=-1, keepdims=True))
        lse = peak + jnp.log(lax.optimization_barrier(jnp.sum(jnp.exp(scores - peak), axis=-1, keepdims=True)))
        probs = jnp.exp(scores - lse)
        probs_low = lax.optimization_barrier(probs.astype(jnp.bfloat16)).astype(jnp.float32)
        attended = jnp.einsum('gjrk,kgd->rgjd', probs_low, value_block).astype(jnp.bfloat16)
        attended_wide = lax.optimization_barrier(attended).astype(jnp.float32)
        delta = jnp.einsum('rgjd,rgjd->gjr', block_gradient, attended_wide)
        dprobs = jnp.einsum('rgjd,kgd->gjrk', block_gradient, value_block)
        dscores = probs * (dprobs - delta[..., None])
        dscores = lax.optimization_barrier(dscores.astype(jnp.bfloat16)).astype(jnp.float32)
        grad_block_query = (jnp.einsum('gjrk,kgd->rgjd', dscores, key_block) * scaling).astype(jnp.bfloat16)
        key_terms = jnp.einsum('gjrk,rgjd->kgd', dscores, current_query_block) * scaling
        value_terms = jnp.einsum('gjrk,rgjd->kgd', probs_low, block_gradient)
        key_gradient = lax.dynamic_update_slice_in_dim(key_gradient, lax.dynamic_slice_in_dim(key_gradient, key_first, window, 0) + key_terms, key_first, 0)
        value_gradient = lax.dynamic_update_slice_in_dim(value_gradient, lax.dynamic_slice_in_dim(value_gradient, key_first, window, 0) + value_terms, key_first, 0)
        return ((key_gradient, value_gradient), (attended.reshape(TOKENS_PER_SHARD, QUERY_HEADS * HEAD_SIZE), grad_block_query.reshape(TOKENS_PER_SHARD, QUERY_HEADS * HEAD_SIZE)))
    empty_gradients = jnp.zeros((PACKED_TOKENS, KEY_VALUE_HEADS, HEAD_SIZE), jnp.float32)
    (key_gradient, value_gradient), (attended, grad_orig) = lax.scan(block_step, (empty_gradients, empty_gradients), jnp.arange(PACKED_TOKENS // TOKENS_PER_SHARD, dtype=jnp.int32))
    slots = jnp.arange(NBLK, dtype=jnp.int32)
    inverse = lax.optimization_barrier(jnp.sum(jnp.where(block_dest[None, :] == slots[:, None], slots[None, :], 0), axis=1)).astype(jnp.int32)
    attention_result = attended.reshape(NBLK, BLK, QUERY_HEADS * HEAD_SIZE)[inverse].reshape(PACKED_TOKENS, QUERY_HEADS * HEAD_SIZE)
    query_gradient = grad_orig.reshape(NBLK, BLK, QUERY_HEADS * HEAD_SIZE)[inverse].reshape(PACKED_TOKENS, QUERY_HEADS * HEAD_SIZE)
    return (attention_result, query_gradient, key_gradient.reshape(PACKED_TOKENS, KEY_VALUE_HEADS * HEAD_SIZE).astype(jnp.bfloat16), value_gradient.reshape(PACKED_TOKENS, KEY_VALUE_HEADS * HEAD_SIZE).astype(jnp.bfloat16))
```

```python
import functools
import math

import jax
import jax.numpy as jnp
from jax import lax
from jax.experimental import pallas as pl
from jax.experimental.pallas import tpu as pltpu
from jax.sharding import PartitionSpec as P

D = 128
BLK = 16
MAX_DOC = 2304
CAP = 2
CHUNK = 4
F32 = jnp.float32
BF16 = jnp.bfloat16


def dot_nt(a, b):
    return lax.dot_general(a, b, (((1,), (1,)), ((), ())), preferred_element_type=F32)


def dot_nn(a, b):
    return lax.dot_general(a, b, (((1,), (0,)), ((), ())), preferred_element_type=F32)


def tables_kernel(n, bpd, me_ref, dest_ref, src_ref, want_ref, count):
    me = me_ref[0]
    for t in range(n * CAP):
        src_ref[t] = 0
    for t in range(n):
        count[t] = 0

    def own_block(b, carry):
        target = dest_ref[me * bpd + b] // bpd
        rank = count[target]
        src_ref[target * CAP + rank] = b
        count[target] = rank + 1
        return carry

    lax.fori_loop(0, bpd, own_block, 0)

    def shard(s, carry):
        def block(b, rank):
            dest = dest_ref[s * bpd + b]
            mine = dest // bpd == me

            @pl.when(mine)
            def _():
                want_ref[dest % bpd] = s * CAP + rank

            return rank + jnp.where(mine, 1, 0)

        lax.fori_loop(0, bpd, block, 0)
        return carry

    lax.fori_loop(0, n, shard, 0)


def main_kernel(
    n,
    pieces,
    lens_ref,
    src_ref,
    want_ref,
    q_ref,
    do_ref,
    k_ref,
    v_ref,
    out_ref,
    dq_ref,
    dk_ref,
    dv_ref,
    kv,
    kt,
    vt,
    bias,
    s_scr,
    p_scr,
    ds_scr,
    acc_k,
    acc_v,
    blocks,
    send,
    g_send,
    g_recv,
    kv_ssem,
    kv_rsem,
    g_ssem,
    g_rsem,
    a_ssem,
    a_rsem,
    *recv,
):
    me = lax.axis_index("ctx")
    tok, width = q_ref.shape
    heads = width // D
    groups = k_ref.shape[1] // D
    per_group = heads // groups
    chunks = heads // CHUNK
    chunks_group = chunks // groups
    bpd = tok // BLK
    scale = 1.0 / math.sqrt(D)
    log2e_scale = scale * math.log2(math.e)

    barrier = pltpu.get_barrier_semaphore()
    for o in range(1, n):
        pl.semaphore_signal(
            barrier,
            inc=1,
            device_id={"ctx": lax.rem(me + o, n)},
            device_id_type=pl.DeviceIdType.MESH,
        )

    for g in range(groups):
        kv[0, g, 0] = k_ref[:, g * D : (g + 1) * D]
        kv[0, g, 1] = v_ref[:, g * D : (g + 1) * D]
    for d in range(1, pieces):

        @pl.when(me < d)
        def _(d=d):
            kv[d] = jnp.zeros_like(kv[d])

    pl.semaphore_wait(barrier, n - 1)

    def kv_copy(d, g):
        return pltpu.make_async_remote_copy(
            src_ref=kv.at[0, g],
            dst_ref=kv.at[d, g],
            send_sem=kv_ssem.at[d, g],
            recv_sem=kv_rsem.at[d, g],
            device_id={"ctx": lax.rem(me + d, n)},
            device_id_type=pl.DeviceIdType.MESH,
        )

    def grad_copy(d, g):
        return pltpu.make_async_remote_copy(
            src_ref=g_send.at[d, g],
            dst_ref=g_recv.at[d, g],
            send_sem=g_ssem.at[d, g],
            recv_sem=g_rsem.at[d, g],
            device_id={"ctx": lax.rem(me + n - d, n)},
            device_id_type=pl.DeviceIdType.MESH,
        )

    for g in range(groups):
        for d in range(1, pieces):

            @pl.when(me + d < n)
            def _(d=d, g=g):
                kv_copy(d, g).start()

    acc_k[...] = jnp.zeros_like(acc_k)
    acc_v[...] = jnp.zeros_like(acc_v)
    query_pos = me * tok + lax.broadcasted_iota(jnp.int32, (1, tok), 1)
    end = jnp.int32(0)
    start = jnp.zeros((1, tok), jnp.int32)
    for doc in range(lens_ref.shape[0]):
        end = end + lens_ref[doc]
        start = start + jnp.where(end <= query_pos, lens_ref[doc], 0)
    for p in range(pieces):
        key_pos = (me - p) * tok + lax.broadcasted_iota(jnp.int32, (tok, tok), 0)
        seen = (key_pos >= start) & (key_pos <= query_pos)
        bias[p] = jnp.where(seen, 0.0, -jnp.inf).astype(F32)

    def fold(x, op):
        return op(x.reshape(tok // 8, 8, tok), axis=0)

    def head_step(ch, g, j):
        h = ch * CHUNK + j
        cols = pl.ds(pl.multiple_of(h * D, D), D)
        q = q_ref[:, cols]
        do = do_ref[:, cols]
        peak = None
        for p in range(pieces):
            s = dot_nt(kv[p, g, 0], q) + bias[p]
            s_scr[p] = s
            top = fold(s, jnp.max)
            peak = top if peak is None else jnp.maximum(peak, top)
        peak = jnp.max(peak, axis=0, keepdims=True)
        total = None
        for p in range(pieces):
            e = jnp.exp2((s_scr[p] - peak) * log2e_scale)
            s_scr[p] = e
            p_scr[p * tok : (p + 1) * tok] = e.astype(BF16)
            part = fold(e, jnp.sum)
            total = part if total is None else total + part
        inv = 1.0 / jnp.sum(total, axis=0, keepdims=True)
        out_t = (dot_nn(vt[g], p_scr[...]) * inv).astype(BF16).astype(F32)
        delta = jnp.sum(out_t * do.astype(F32).T, axis=0, keepdims=True)
        lanes = pl.ds(pl.multiple_of(j * D, D), D)
        blocks[0, :, :, lanes] = out_t.T.astype(BF16).reshape(bpd, BLK, D)
        for p in range(pieces):
            dp = dot_nt(kv[p, g, 1], do)
            pn = s_scr[p] * inv
            ds = (pn * (dp - delta)).astype(BF16)
            ds_scr[p * tok : (p + 1) * tok] = ds
            acc_v[g, p] += dot_nn(pn.astype(BF16), do)
            acc_k[g, p] += dot_nn(ds, q)
        dq_t = dot_nn(kt[g], ds_scr[...]) * scale
        blocks[1, :, :, lanes] = dq_t.T.astype(BF16).reshape(bpd, BLK, D)

    def block_copy(ch, o):
        target = lax.rem(me + o, n)
        return pltpu.make_async_remote_copy(
            src_ref=send.at[ch, target],
            dst_ref=recv[ch].at[me],
            send_sem=a_ssem.at[ch],
            recv_sem=a_rsem.at[ch],
            device_id={"ctx": target},
            device_id_type=pl.DeviceIdType.MESH,
        )

    def chunk_step(ch, carry):
        g = ch // chunks_group
        first = lax.rem(ch, chunks_group) == 0
        last = lax.rem(ch, chunks_group) == chunks_group - 1

        @pl.when(first)
        def _():
            for d in range(pieces):
                if d > 0:

                    @pl.when(me >= d)
                    def _(d=d):
                        kv_copy(d, g).wait_recv()

                kt[g, :, d * tok : (d + 1) * tok] = kv[d, g, 0].astype(F32).T.astype(BF16)
                vt[g, :, d * tok : (d + 1) * tok] = kv[d, g, 1].astype(F32).T.astype(BF16)

        def one_head(j, inner):
            head_step(ch, g, j)
            return inner

        lax.fori_loop(0, CHUNK, one_head, 0)

        for t in range(n):
            for c in range(CAP):
                b = src_ref[t * CAP + c]
                send[ch, t, c, 0] = blocks[0, b]
                send[ch, t, c, 1] = blocks[1, b]
        for cc in range(chunks):

            @pl.when(ch == cc)
            def _(cc=cc):
                recv[cc][me] = send[cc, me]
                for o in range(1, n):
                    block_copy(cc, o).start()

        @pl.when(last)
        def _():
            for d in range(1, pieces):

                @pl.when(me >= d)
                def _(d=d):
                    g_send[d, g, 0] = acc_k[g, d].astype(BF16)
                    g_send[d, g, 1] = acc_v[g, d].astype(BF16)
                    grad_copy(d, g).start()

        return carry

    lax.fori_loop(0, chunks, chunk_step, 0)

    for ch in range(chunks):
        held = recv[ch].at[pl.ds(0, n - 1)]
        pltpu.make_async_copy(held, held, a_rsem.at[ch]).wait()
        for slot in range(bpd):
            w = want_ref[slot]
            rows = slice(slot * BLK, (slot + 1) * BLK)
            cols = slice(ch * CHUNK * D, (ch + 1) * CHUNK * D)
            out_ref[rows, cols] = recv[ch][w // CAP, w % CAP, 0]
            dq_ref[rows, cols] = recv[ch][w // CAP, w % CAP, 1]

    for g in range(groups):
        for d in range(1, pieces):

            @pl.when(me + d < n)
            def _(d=d, g=g):
                grad_copy(d, g).wait_recv()
                acc_k[g, 0] += g_recv[d, g, 0].astype(F32)
                acc_v[g, 0] += g_recv[d, g, 1].astype(F32)

        dk_ref[:, g * D : (g + 1) * D] = (acc_k[g, 0] * scale).astype(BF16)
        dv_ref[:, g * D : (g + 1) * D] = acc_v[g, 0].astype(BF16)

    for ch in range(chunks):
        sent = send.at[ch, pl.ds(0, n - 1)]
        pltpu.make_async_copy(sent, sent, a_ssem.at[ch]).wait()
    for g in range(groups):
        for d in range(1, pieces):

            @pl.when(me + d < n)
            def _(d=d, g=g):
                kv_copy(d, g).wait_send()

            @pl.when(me >= d)
            def _(d=d, g=g):
                grad_copy(d, g).wait_send()


def shards(q, k, v, do, lens, dest):
    n = lax.axis_size("ctx")
    tok, width = q.shape
    heads = width // D
    groups = k.shape[1] // D
    bpd = tok // BLK
    pieces = min(n, (MAX_DOC - 1 + tok - 1) // tok + 1)
    chunks = heads // CHUNK
    keys = pieces * tok
    smem = pl.BlockSpec(memory_space=pltpu.SMEM)
    vmem = pl.BlockSpec(memory_space=pltpu.VMEM)
    me = lax.axis_index("ctx").astype(jnp.int32).reshape(1)
    src, want = pl.pallas_call(
        functools.partial(tables_kernel, n, bpd),
        out_shape=(
            jax.ShapeDtypeStruct((n * CAP,), jnp.int32),
            jax.ShapeDtypeStruct((bpd,), jnp.int32),
        ),
        in_specs=[smem, smem],
        out_specs=(smem, smem),
        scratch_shapes=[pltpu.SMEM((n,), jnp.int32)],
    )(me, dest)
    return pl.pallas_call(
        functools.partial(main_kernel, n, pieces),
        out_shape=(
            jax.ShapeDtypeStruct(q.shape, BF16),
            jax.ShapeDtypeStruct(q.shape, BF16),
            jax.ShapeDtypeStruct(k.shape, BF16),
            jax.ShapeDtypeStruct(v.shape, BF16),
        ),
        in_specs=[smem, smem, smem, vmem, vmem, vmem, vmem],
        out_specs=(vmem, vmem, vmem, vmem),
        scratch_shapes=[
            pltpu.VMEM((pieces, groups, 2, tok, D), BF16),
            pltpu.VMEM((groups, D, keys), BF16),
            pltpu.VMEM((groups, D, keys), BF16),
            pltpu.VMEM((pieces, tok, tok), F32),
            pltpu.VMEM((pieces, tok, tok), F32),
            pltpu.VMEM((keys, tok), BF16),
            pltpu.VMEM((keys, tok), BF16),
            pltpu.VMEM((groups, pieces, tok, D), F32),
            pltpu.VMEM((groups, pieces, tok, D), F32),
            pltpu.VMEM((2, bpd, BLK, CHUNK * D), BF16),
            pltpu.VMEM((chunks, n, CAP, 2, BLK, CHUNK * D), BF16),
            pltpu.VMEM((pieces, groups, 2, tok, D), BF16),
            pltpu.VMEM((pieces, groups, 2, tok, D), BF16),
            pltpu.SemaphoreType.DMA((pieces, groups)),
            pltpu.SemaphoreType.DMA((pieces, groups)),
            pltpu.SemaphoreType.DMA((pieces, groups)),
            pltpu.SemaphoreType.DMA((pieces, groups)),
            pltpu.SemaphoreType.DMA((chunks,)),
            pltpu.SemaphoreType.DMA((chunks,)),
        ]
        + [pltpu.VMEM((n, CAP, 2, BLK, CHUNK * D), BF16)] * chunks,
        compiler_params=pltpu.CompilerParams(
            collective_id=0, has_side_effects=True, vmem_limit_bytes=60 * 2**20
        ),
    )(lens, src, want, q, do, k, v)


def solution(mesh):
    rows = P(("dp", "ctx"), "head")
    return jax.shard_map(
        shards,
        mesh=mesh,
        in_specs=(rows, rows, rows, rows, P("dp"), P("dp")),
        out_specs=(rows, rows, rows, rows),
        check_vma=False,
    )
```

```python
import functools
import math

import jax
import jax.numpy as jnp
from jax import lax
from jax.experimental import pallas as pl
from jax.experimental.pallas import tpu as pltpu
from jax.sharding import PartitionSpec as P

D = 128
BLK = 16
MAX_DOC = 2304
CAP = 2
CHUNK = 2
ROW = 4
F32 = jnp.float32
BF16 = jnp.bfloat16


def dot_nt(a, b):
    return lax.dot_general(a, b, (((1,), (1,)), ((), ())), preferred_element_type=F32)


def dot_nn(a, b):
    return lax.dot_general(a, b, (((1,), (0,)), ((), ())), preferred_element_type=F32)


def main_kernel(
    n,
    pieces,
    lens_ref,
    dest_ref,
    q_ref,
    do_ref,
    k_ref,
    v_ref,
    out_ref,
    dq_ref,
    dk_ref,
    dv_ref,
    kv,
    kt,
    vt,
    bias,
    s_scr,
    p_scr,
    ds_scr,
    acc_k,
    acc_v,
    blocks,
    send,
    g_send,
    g_recv,
    kv_ssem,
    kv_rsem,
    g_ssem,
    g_rsem,
    a_ssem,
    a_rsem,
    tab_v,
    tab_s,
    tab_sem,
    *recv,
):
    me = lax.axis_index("ctx")
    tok, width = q_ref.shape
    heads = width // D
    groups = k_ref.shape[1] // D
    per_group = heads // groups
    chunks = heads // CHUNK
    chunks_group = chunks // groups
    bpd = tok // BLK
    scale = 1.0 / math.sqrt(D)
    log2e_scale = scale * math.log2(math.e)

    barrier = pltpu.get_barrier_semaphore()
    for o in range(1, n):
        pl.semaphore_signal(
            barrier,
            inc=1,
            device_id={"ctx": lax.rem(me + o, n)},
            device_id_type=pl.DeviceIdType.MESH,
        )

    x, y = me // ROW, lax.rem(me, ROW)
    opp = lax.rem(y + ROW // 2, ROW)
    n_rows = n // ROW
    base = ROW - 1
    for g in range(groups):
        kv[base, g, 0] = k_ref[:, g * D : (g + 1) * D]
        kv[base, g, 1] = v_ref[:, g * D : (g + 1) * D]
    for d in range(1, pieces):

        @pl.when(me < d)
        def _(d=d):
            kv[base + d] = jnp.zeros_like(kv[base + d])

    pl.semaphore_wait(barrier, n - 1)

    def hop(g, message, src, dst, dx, ty, go):
        @pl.when(go)
        def _():
            pltpu.make_async_remote_copy(
                src_ref=kv.at[base + src, g],
                dst_ref=kv.at[base + dst, g],
                send_sem=kv_ssem.at[message, g],
                recv_sem=kv_rsem.at[base + dst, g],
                device_id={"ctx": (x + dx) * ROW + ty},
                device_id_type=pl.DeviceIdType.MESH,
            ).start()

    def drain(g, message, go):
        @pl.when(go)
        def _():
            held = kv.at[base, g]
            pltpu.make_async_copy(held, held, kv_ssem.at[message, g]).wait()

    def arrive(g, d, go):
        @pl.when(go)
        def _():
            held = kv.at[base + d, g]
            pltpu.make_async_copy(held, held, kv_rsem.at[base + d, g]).wait()

    def beside(k):
        return lax.rem(y + k, ROW)

    below = x < n_rows - 1
    third = (y == ROW - 1) & (x + 3 < n_rows)
    row_go = {k: (beside(k) > y) | (below if k == ROW // 2 else (y < 0)) for k in range(1, ROW)}
    far_opp = (x >= 1) & below & (2 * ROW + y - opp < pieces)
    far_go = {k: (x >= 2) & (2 * ROW + beside(k) - y < pieces) for k in (1, ROW - 1)}

    def stage_one(g):
        hop(g, 0, 0, ROW, 1, y, below)
        for k in range(1, ROW):
            hop(g, k, 0, beside(k) - y, 0, beside(k), row_go[k])
        hop(g, ROW, 0, 3 * ROW - y, 3, 0, third)

    def stage_two(g):
        arrive(g, ROW, x >= 1)
        hop(g, 5, ROW, 2 * ROW, 1, y, (x >= 1) & below)
        hop(g, 6, ROW, ROW + beside(1) - y, 0, beside(1), x >= 1)
        hop(g, 7, ROW, ROW + beside(ROW - 1) - y, 0, beside(ROW - 1), x >= 1)
        arrive(g, y - opp, below | (y > opp))
        hop(g, 8, y - opp, ROW + y - opp, 1, y, below)

    def stage_three(g):
        arrive(g, 2 * ROW, x >= 2)
        hop(g, 9, 2 * ROW, 2 * ROW + beside(1) - y, 0, beside(1), far_go[1])
        hop(g, 10, 2 * ROW, 2 * ROW + beside(ROW - 1) - y, 0, beside(ROW - 1), far_go[ROW - 1])
        arrive(g, ROW + y - opp, x >= 1)
        hop(g, 11, ROW + y - opp, 2 * ROW + y - opp, 1, y, far_opp)

    def stage_last(g):
        for k in (1, ROW - 1):
            side = beside(k)
            arrive(g, y - side, side < y)
            arrive(g, ROW + y - side, x >= 1)
            arrive(g, 2 * ROW + y - side, (x >= 2) & (2 * ROW + y - side < pieces))
        arrive(g, 2 * ROW + y - opp, (x >= 2) & (2 * ROW + y - opp < pieces))
        arrive(g, 2 * ROW + 1, (x >= 3) & (y == 0))

    def stage_sent(g):
        drain(g, 0, below)
        for k in range(1, ROW):
            drain(g, k, row_go[k])
        drain(g, ROW, third)
        drain(g, 5, (x >= 1) & below)
        drain(g, 6, x >= 1)
        drain(g, 7, x >= 1)
        drain(g, 8, below)
        drain(g, 9, far_go[1])
        drain(g, 10, far_go[ROW - 1])
        drain(g, 11, far_opp)

    def grad_copy(d, g):
        return pltpu.make_async_remote_copy(
            src_ref=g_send.at[d, g],
            dst_ref=g_recv.at[d, g],
            send_sem=g_ssem.at[d, g],
            recv_sem=g_rsem.at[d, g],
            device_id={"ctx": lax.rem(me + n - d, n)},
            device_id_type=pl.DeviceIdType.MESH,
        )

    stage_one(0)

    nb = n * bpd
    lane = lax.broadcasted_iota(jnp.int32, (nb, nb), 1)
    sub = lax.broadcasted_iota(jnp.int32, (nb, nb), 0)
    dest_row = jnp.broadcast_to(dest_ref[...], (nb, nb))
    dest_col = dest_row.T
    same = (dest_row // bpd == dest_col // bpd) & (lane // bpd == sub // bpd) & (lane < sub)
    rank = jnp.sum(jnp.where(same, 1.0, 0.0).astype(F32), axis=1, keepdims=True).astype(jnp.int32)
    slot = (dest_col // bpd) * CAP + rank
    picked = (sub // bpd == me) & (slot == lane)
    src_row = jnp.sum(jnp.where(picked, sub - me * bpd, 0), axis=0, keepdims=True)
    tab_v[0:1] = jnp.clip(src_row, 0, bpd - 1)
    found = dest_col == me * bpd + lane
    want_row = jnp.sum(jnp.where(found, (sub // bpd) * CAP + rank, 0), axis=0, keepdims=True)
    tab_v[1:2] = jnp.clip(want_row, 0, n * CAP - 1)
    to_smem = pltpu.make_async_copy(tab_v, tab_s, tab_sem)
    to_smem.start()

    acc_k[...] = jnp.zeros_like(acc_k)
    acc_v[...] = jnp.zeros_like(acc_v)
    query_pos = me * tok + lax.broadcasted_iota(jnp.int32, (1, tok), 1)
    end = jnp.int32(0)
    start = jnp.zeros((1, tok), jnp.int32)
    for doc in range(lens_ref.shape[0]):
        end = end + lens_ref[doc]
        start = start + jnp.where(end <= query_pos, lens_ref[doc], 0)
    for p in range(pieces):
        key_pos = (me - p) * tok + lax.broadcasted_iota(jnp.int32, (tok, tok), 0)
        seen = (key_pos >= start) & (key_pos <= query_pos)
        bias[p] = jnp.where(seen, 0.0, -jnp.inf).astype(F32)

    to_smem.wait()
    stage_two(0)
    stage_three(0)
    for g in range(1, groups):
        stage_one(g)

    def fold(x, op):
        return op(x.reshape(tok // 8, 8, tok), axis=0)

    def head_step(ch, g, j):
        h = ch * CHUNK + j
        cols = pl.ds(pl.multiple_of(h * D, D), D)
        q = q_ref[:, cols]
        do = do_ref[:, cols]
        peak = None
        for p in range(pieces):
            s = dot_nt(kv[base + p, g, 0], q) + bias[p]
            s_scr[p] = s
            top = fold(s, jnp.max)
            peak = top if peak is None else jnp.maximum(peak, top)
        peak = jnp.max(peak, axis=0, keepdims=True)
        total = None
        for p in range(pieces):
            e = jnp.exp2((s_scr[p] - peak) * log2e_scale)
            s_scr[p] = e
            p_scr[p * tok : (p + 1) * tok] = e.astype(BF16)
            part = fold(e, jnp.sum)
            total = part if total is None else total + part
        inv = 1.0 / jnp.sum(total, axis=0, keepdims=True)
        out_t = (dot_nn(vt[g], p_scr[...]) * inv).astype(BF16).astype(F32)
        delta = jnp.sum(out_t * do.astype(F32).T, axis=0, keepdims=True)
        lanes = pl.ds(pl.multiple_of(j * D, D), D)
        blocks[0, :, :, lanes] = out_t.T.astype(BF16).reshape(bpd, BLK, D)
        for p in range(pieces):
            dp = dot_nt(kv[base + p, g, 1], do)
            pn = s_scr[p] * inv
            ds = (pn * (dp - delta)).astype(BF16)
            ds_scr[p * tok : (p + 1) * tok] = ds
            acc_v[g, p] += dot_nn(pn.astype(BF16), do)
            acc_k[g, p] += dot_nn(ds, q)
        dq_t = dot_nn(kt[g], ds_scr[...]) * scale
        blocks[1, :, :, lanes] = dq_t.T.astype(BF16).reshape(bpd, BLK, D)

    def block_copy(ch, o):
        target = lax.rem(me + o, n)
        return pltpu.make_async_remote_copy(
            src_ref=send.at[ch, target],
            dst_ref=recv[ch].at[me],
            send_sem=a_ssem.at[ch],
            recv_sem=a_rsem.at[ch],
            device_id={"ctx": target},
            device_id_type=pl.DeviceIdType.MESH,
        )

    def chunk_step(ch, carry):
        g = ch // chunks_group
        first = lax.rem(ch, chunks_group) == 0
        last = lax.rem(ch, chunks_group) == chunks_group - 1

        @pl.when(first)
        def _():
            stage_last(g)
            for d in range(pieces):
                kt[g, :, d * tok : (d + 1) * tok] = kv[base + d, g, 0].astype(F32).T.astype(BF16)
                vt[g, :, d * tok : (d + 1) * tok] = kv[base + d, g, 1].astype(F32).T.astype(BF16)

        def one_head(j, inner):
            head_step(ch, g, j)
            return inner

        lax.fori_loop(0, CHUNK, one_head, 0)

        for t in range(n):
            for c in range(CAP):
                b = tab_s[0, t * CAP + c]
                send[ch, t, c, 0] = blocks[0, b]
                send[ch, t, c, 1] = blocks[1, b]
        for cc in range(chunks):

            @pl.when(ch == cc)
            def _(cc=cc):
                recv[cc][me] = send[cc, me]
                for o in range(1, n):
                    block_copy(cc, o).start()

        for g2 in range(1, groups):

            @pl.when(ch == (g2 - 1) * chunks_group)
            def _(g2=g2):
                stage_two(g2)

            @pl.when(ch == (g2 - 1) * chunks_group + 1)
            def _(g2=g2):
                stage_three(g2)

        @pl.when(last)
        def _():
            for d in range(1, pieces):

                @pl.when(me >= d)
                def _(d=d):
                    g_send[d, g, 0] = acc_k[g, d].astype(BF16)
                    g_send[d, g, 1] = acc_v[g, d].astype(BF16)
                    grad_copy(d, g).start()

        return carry

    lax.fori_loop(0, chunks, chunk_step, 0)

    for ch in range(chunks):
        held = recv[ch].at[pl.ds(0, n - 1)]
        pltpu.make_async_copy(held, held, a_rsem.at[ch]).wait()
        for slot in range(bpd):
            w = tab_s[1, slot]
            rows = slice(slot * BLK, (slot + 1) * BLK)
            cols = slice(ch * CHUNK * D, (ch + 1) * CHUNK * D)
            out_ref[rows, cols] = recv[ch][w // CAP, w % CAP, 0]
            dq_ref[rows, cols] = recv[ch][w // CAP, w % CAP, 1]

    for g in range(groups):
        for d in range(1, pieces):

            @pl.when(me + d < n)
            def _(d=d, g=g):
                grad_copy(d, g).wait_recv()
                acc_k[g, 0] += g_recv[d, g, 0].astype(F32)
                acc_v[g, 0] += g_recv[d, g, 1].astype(F32)

        dk_ref[:, g * D : (g + 1) * D] = (acc_k[g, 0] * scale).astype(BF16)
        dv_ref[:, g * D : (g + 1) * D] = acc_v[g, 0].astype(BF16)

    for ch in range(chunks):
        sent = send.at[ch, pl.ds(0, n - 1)]
        pltpu.make_async_copy(sent, sent, a_ssem.at[ch]).wait()
    for g in range(groups):
        stage_sent(g)
        for d in range(1, pieces):

            @pl.when(me >= d)
            def _(d=d, g=g):
                grad_copy(d, g).wait_send()


def shards(q, k, v, do, lens, dest):
    n = lax.axis_size("ctx")
    tok, width = q.shape
    heads = width // D
    groups = k.shape[1] // D
    bpd = tok // BLK
    pieces = min(n, (MAX_DOC - 1 + tok - 1) // tok + 1)
    chunks = heads // CHUNK
    keys = pieces * tok
    smem = pl.BlockSpec(memory_space=pltpu.SMEM)
    vmem = pl.BlockSpec(memory_space=pltpu.VMEM)
    return pl.pallas_call(
        functools.partial(main_kernel, n, pieces),
        out_shape=(
            jax.ShapeDtypeStruct(q.shape, BF16),
            jax.ShapeDtypeStruct(q.shape, BF16),
            jax.ShapeDtypeStruct(k.shape, BF16),
            jax.ShapeDtypeStruct(v.shape, BF16),
        ),
        in_specs=[smem, vmem, vmem, vmem, vmem, vmem],
        out_specs=(vmem, vmem, vmem, vmem),
        scratch_shapes=[
            pltpu.VMEM((4 * ROW - 1, groups, 2, tok, D), BF16),
            pltpu.VMEM((groups, D, keys), BF16),
            pltpu.VMEM((groups, D, keys), BF16),
            pltpu.VMEM((pieces, tok, tok), F32),
            pltpu.VMEM((pieces, tok, tok), F32),
            pltpu.VMEM((keys, tok), BF16),
            pltpu.VMEM((keys, tok), BF16),
            pltpu.VMEM((groups, pieces, tok, D), F32),
            pltpu.VMEM((groups, pieces, tok, D), F32),
            pltpu.VMEM((2, bpd, BLK, CHUNK * D), BF16),
            pltpu.VMEM((chunks, n, CAP, 2, BLK, CHUNK * D), BF16),
            pltpu.VMEM((pieces, groups, 2, tok, D), BF16),
            pltpu.VMEM((pieces, groups, 2, tok, D), BF16),
            pltpu.SemaphoreType.DMA((3 * ROW, groups)),
            pltpu.SemaphoreType.DMA((4 * ROW - 1, groups)),
            pltpu.SemaphoreType.DMA((pieces, groups)),
            pltpu.SemaphoreType.DMA((pieces, groups)),
            pltpu.SemaphoreType.DMA((chunks,)),
            pltpu.SemaphoreType.DMA((chunks,)),
            pltpu.VMEM((2, n * bpd), jnp.int32),
            pltpu.SMEM((2, n * bpd), jnp.int32),
            pltpu.SemaphoreType.DMA(()),
        ]
        + [pltpu.VMEM((n, CAP, 2, BLK, CHUNK * D), BF16)] * chunks,
        compiler_params=pltpu.CompilerParams(
            collective_id=0, has_side_effects=True, vmem_limit_bytes=60 * 2**20
        ),
    )(lens, dest.reshape(1, n * bpd), q, do, k, v)


def solution(mesh):
    rows = P(("dp", "ctx"), "head")
    return jax.shard_map(
        shards,
        mesh=mesh,
        in_specs=(rows, rows, rows, rows, P("dp"), P("dp")),
        out_specs=(rows, rows, rows, rows),
        check_vma=False,
    )
```

```python
import functools
import math

import jax
import jax.numpy as jnp
from jax import lax
from jax.experimental import pallas as pl
from jax.experimental.pallas import tpu as pltpu
from jax.sharding import PartitionSpec as P

D = 128
BLK = 16
MAX_DOC = 2304
CAP = 2
CHUNK = 2
ROW = 4
F32 = jnp.float32
BF16 = jnp.bfloat16


def dot_nt(a, b):
    return lax.dot_general(a, b, (((1,), (1,)), ((), ())), preferred_element_type=F32)


def dot_nn(a, b):
    return lax.dot_general(a, b, (((1,), (0,)), ((), ())), preferred_element_type=F32)


def main_kernel(
    n,
    pieces,
    lens_ref,
    dest_ref,
    q_ref,
    do_ref,
    k_ref,
    v_ref,
    out_ref,
    dq_ref,
    dk_ref,
    dv_ref,
    kv,
    kt,
    vt,
    bias,
    s_scr,
    p_scr,
    ds_scr,
    acc_k,
    acc_v,
    blocks,
    send,
    g_send,
    g_recv,
    kv_ssem,
    kv_rsem,
    g_ssem,
    g_rsem,
    a_ssem,
    a_rsem,
    tab_v,
    tab_s,
    tab_sem,
    *recv,
):
    me = lax.axis_index("ctx")
    tok, width = q_ref.shape
    heads = width // D
    groups = k_ref.shape[1] // D
    per_group = heads // groups
    chunks = heads // CHUNK
    chunks_group = chunks // groups
    bpd = tok // BLK
    scale = 1.0 / math.sqrt(D)
    log2e_scale = scale * math.log2(math.e)

    barrier = pltpu.get_barrier_semaphore()
    for o in range(1, n):
        pl.semaphore_signal(
            barrier,
            inc=1,
            device_id={"ctx": lax.rem(me + o, n)},
            device_id_type=pl.DeviceIdType.MESH,
        )

    x, y = me // ROW, lax.rem(me, ROW)
    opp = lax.rem(y + ROW // 2, ROW)
    n_rows = n // ROW
    base = ROW - 1
    for g in range(groups):
        kv[base, g, 0] = k_ref[:, g * D : (g + 1) * D]
        kv[base, g, 1] = v_ref[:, g * D : (g + 1) * D]
    for d in range(1, pieces):

        @pl.when(me < d)
        def _(d=d):
            kv[base + d] = jnp.zeros_like(kv[base + d])

    pl.semaphore_wait(barrier, n - 1)

    def hop(g, message, src, dst, dx, ty, go):
        @pl.when(go)
        def _():
            pltpu.make_async_remote_copy(
                src_ref=kv.at[base + src, g],
                dst_ref=kv.at[base + dst, g],
                send_sem=kv_ssem.at[message, g],
                recv_sem=kv_rsem.at[base + dst, g],
                device_id={"ctx": (x + dx) * ROW + ty},
                device_id_type=pl.DeviceIdType.MESH,
            ).start()

    def drain(g, message, go):
        @pl.when(go)
        def _():
            held = kv.at[base, g]
            pltpu.make_async_copy(held, held, kv_ssem.at[message, g]).wait()

    def arrive(g, d, go):
        @pl.when(go)
        def _():
            held = kv.at[base + d, g]
            pltpu.make_async_copy(held, held, kv_rsem.at[base + d, g]).wait()

    def beside(k):
        return lax.rem(y + k, ROW)

    below = x < n_rows - 1
    third = (y == ROW - 1) & (x + 3 < n_rows)
    row_go = {k: (beside(k) > y) | (below if k == ROW // 2 else (y < 0)) for k in range(1, ROW)}
    far_opp = (x >= 1) & below & (2 * ROW + y - opp < pieces)
    far_go = {k: (x >= 2) & (2 * ROW + beside(k) - y < pieces) for k in (1, ROW - 1)}

    def stage_one(g):
        hop(g, 0, 0, ROW, 1, y, below)
        for k in range(1, ROW):
            hop(g, k, 0, beside(k) - y, 0, beside(k), row_go[k])
        hop(g, ROW, 0, 3 * ROW - y, 3, 0, third)

    def stage_two(g):
        arrive(g, ROW, x >= 1)
        hop(g, 5, ROW, 2 * ROW, 1, y, (x >= 1) & below)
        hop(g, 6, ROW, ROW + beside(1) - y, 0, beside(1), x >= 1)
        hop(g, 7, ROW, ROW + beside(ROW - 1) - y, 0, beside(ROW - 1), x >= 1)
        arrive(g, y - opp, below | (y > opp))
        hop(g, 8, y - opp, ROW + y - opp, 1, y, below)

    def stage_three(g):
        arrive(g, 2 * ROW, x >= 2)
        hop(g, 9, 2 * ROW, 2 * ROW + beside(1) - y, 0, beside(1), far_go[1])
        hop(g, 10, 2 * ROW, 2 * ROW + beside(ROW - 1) - y, 0, beside(ROW - 1), far_go[ROW - 1])
        arrive(g, ROW + y - opp, x >= 1)
        hop(g, 11, ROW + y - opp, 2 * ROW + y - opp, 1, y, far_opp)

    def stage_last(g):
        for k in (1, ROW - 1):
            side = beside(k)
            arrive(g, y - side, side < y)
            arrive(g, ROW + y - side, x >= 1)
            arrive(g, 2 * ROW + y - side, (x >= 2) & (2 * ROW + y - side < pieces))
        arrive(g, 2 * ROW + y - opp, (x >= 2) & (2 * ROW + y - opp < pieces))
        arrive(g, 2 * ROW + 1, (x >= 3) & (y == 0))

    def stage_sent(g):
        drain(g, 0, below)
        for k in range(1, ROW):
            drain(g, k, row_go[k])
        drain(g, ROW, third)
        drain(g, 5, (x >= 1) & below)
        drain(g, 6, x >= 1)
        drain(g, 7, x >= 1)
        drain(g, 8, below)
        drain(g, 9, far_go[1])
        drain(g, 10, far_go[ROW - 1])
        drain(g, 11, far_opp)

    def put(g, message, d):
        g_send[message, g, 0] = acc_k[g, d].astype(BF16)
        g_send[message, g, 1] = acc_v[g, d].astype(BF16)

    def ship(g, message, dx, ty):
        pltpu.make_async_remote_copy(
            src_ref=g_send.at[message, g],
            dst_ref=g_recv.at[message, g],
            send_sem=g_ssem.at[message, g],
            recv_sem=g_rsem.at[message, g],
            device_id={"ctx": (x - dx) * ROW + ty},
            device_id_type=pl.DeviceIdType.MESH,
        ).start()

    def give(g, message, d, dx, ty, go):
        @pl.when(go)
        def _():
            put(g, message, d)
            ship(g, message, dx, ty)

    def landed(g, message):
        held = g_recv.at[message, g]
        pltpu.make_async_copy(held, held, g_rsem.at[message, g]).wait()

    def take(g, message, d, go):
        @pl.when(go)
        def _():
            landed(g, message)
            acc_k[g, d] += g_recv[message, g, 0].astype(F32)
            acc_v[g, d] += g_recv[message, g, 1].astype(F32)

    nxt, prv = beside(1), beside(ROW - 1)
    opp_go = below | (opp < y)
    gives = [
        (x >= 2) & (2 * ROW + y - nxt < pieces),
        (x >= 2) & (2 * ROW + y - prv < pieces),
        x >= 1,
        x >= 1,
        (x >= 2) & (2 * ROW + y - opp < pieces),
        nxt < y,
        prv < y,
        (x >= 3) & (y == 0),
        x >= 2,
        x >= 1,
        x >= 1,
        opp_go,
    ]

    def reduce_one(g):
        give(g, 0, 2 * ROW + y - nxt, 0, nxt, gives[0])
        give(g, 1, 2 * ROW + y - prv, 0, prv, gives[1])
        give(g, 4, 2 * ROW + y - opp, 1, y, gives[4])
        give(g, 7, 2 * ROW + 1, 3, ROW - 1, gives[7])
        give(g, 2, ROW + y - nxt, 0, nxt, gives[2])
        give(g, 3, ROW + y - prv, 0, prv, gives[3])
        give(g, 5, y - nxt, 0, nxt, gives[5])
        give(g, 6, y - prv, 0, prv, gives[6])

    def reduce_two(g):
        take(g, 0, 2 * ROW, (x >= 2) & (2 * ROW + prv - y < pieces))
        take(g, 1, 2 * ROW, (x >= 2) & (2 * ROW + nxt - y < pieces))
        give(g, 8, 2 * ROW, 1, y, gives[8])

    def reduce_three(g):
        take(g, 4, ROW + y - opp, (x >= 1) & below & (2 * ROW + y - opp < pieces))
        give(g, 10, ROW + y - opp, 1, y, gives[10])
        take(g, 2, ROW, x >= 1)
        take(g, 3, ROW, x >= 1)
        take(g, 8, ROW, (x >= 1) & below)
        give(g, 9, ROW, 1, y, gives[9])

    def reduce_four(g):
        @pl.when(opp < y)
        def _():
            @pl.when(below)
            def _():
                landed(g, 10)
                acc_k[g, y - opp] += g_recv[10, g, 0].astype(F32)
                acc_v[g, y - opp] += g_recv[10, g, 1].astype(F32)

            put(g, 11, y - opp)

        @pl.when((opp > y) & below)
        def _():
            landed(g, 10)
            g_send[11, g] = g_recv[10, g]

        @pl.when(opp_go)
        def _():
            ship(g, 11, 0, opp)

    def reduce_last(g):
        take(g, 5, 0, y < prv)
        take(g, 6, 0, y < nxt)
        take(g, 7, 0, (y == ROW - 1) & (x + 3 < n_rows))
        take(g, 9, 0, below)
        take(g, 11, 0, below | (y < opp))
        dk_ref[:, g * D : (g + 1) * D] = (acc_k[g, 0] * scale).astype(BF16)
        dv_ref[:, g * D : (g + 1) * D] = acc_v[g, 0].astype(BF16)

    def reduce_sent(g):
        for message, go in enumerate(gives):

            @pl.when(go)
            def _(message=message):
                held = g_send.at[message, g]
                pltpu.make_async_copy(held, held, g_ssem.at[message, g]).wait()

    stage_one(0)

    nb = n * bpd
    lane = lax.broadcasted_iota(jnp.int32, (nb, nb), 1)
    sub = lax.broadcasted_iota(jnp.int32, (nb, nb), 0)
    dest_row = jnp.broadcast_to(dest_ref[...], (nb, nb))
    dest_col = dest_row.T
    same = (dest_row // bpd == dest_col // bpd) & (lane // bpd == sub // bpd) & (lane < sub)
    rank = jnp.sum(jnp.where(same, 1.0, 0.0).astype(F32), axis=1, keepdims=True).astype(jnp.int32)
    slot = (dest_col // bpd) * CAP + rank
    picked = (sub // bpd == me) & (slot == lane)
    src_row = jnp.sum(jnp.where(picked, sub - me * bpd, 0), axis=0, keepdims=True)
    tab_v[0:1] = jnp.clip(src_row, 0, bpd - 1)
    found = dest_col == me * bpd + lane
    want_row = jnp.sum(jnp.where(found, (sub // bpd) * CAP + rank, 0), axis=0, keepdims=True)
    tab_v[1:2] = jnp.clip(want_row, 0, n * CAP - 1)
    to_smem = pltpu.make_async_copy(tab_v, tab_s, tab_sem)
    to_smem.start()

    acc_k[...] = jnp.zeros_like(acc_k)
    acc_v[...] = jnp.zeros_like(acc_v)
    query_pos = me * tok + lax.broadcasted_iota(jnp.int32, (1, tok), 1)
    end = jnp.int32(0)
    start = jnp.zeros((1, tok), jnp.int32)
    for doc in range(lens_ref.shape[0]):
        end = end + lens_ref[doc]
        start = start + jnp.where(end <= query_pos, lens_ref[doc], 0)
    for p in range(pieces):
        key_pos = (me - p) * tok + lax.broadcasted_iota(jnp.int32, (tok, tok), 0)
        seen = (key_pos >= start) & (key_pos <= query_pos)
        bias[p] = jnp.where(seen, 0.0, -jnp.inf).astype(F32)

    to_smem.wait()
    stage_two(0)
    stage_three(0)
    for g in range(1, groups):
        stage_one(g)

    def fold(x, op):
        return op(x.reshape(tok // 8, 8, tok), axis=0)

    def head_step(ch, g, j):
        h = ch * CHUNK + j
        cols = pl.ds(pl.multiple_of(h * D, D), D)
        q = q_ref[:, cols]
        do = do_ref[:, cols]
        peak = None
        for p in range(pieces):
            s = dot_nt(kv[base + p, g, 0], q) + bias[p]
            s_scr[p] = s
            top = fold(s, jnp.max)
            peak = top if peak is None else jnp.maximum(peak, top)
        peak = jnp.max(peak, axis=0, keepdims=True)
        total = None
        for p in range(pieces):
            e = jnp.exp2((s_scr[p] - peak) * log2e_scale)
            s_scr[p] = e
            p_scr[p * tok : (p + 1) * tok] = e.astype(BF16)
            part = fold(e, jnp.sum)
            total = part if total is None else total + part
        inv = 1.0 / jnp.sum(total, axis=0, keepdims=True)
        out_t = (dot_nn(vt[g], p_scr[...]) * inv).astype(BF16).astype(F32)
        delta = jnp.sum(out_t * do.astype(F32).T, axis=0, keepdims=True)
        lanes = pl.ds(pl.multiple_of(j * D, D), D)
        blocks[0, :, :, lanes] = out_t.T.astype(BF16).reshape(bpd, BLK, D)
        for p in range(pieces):
            dp = dot_nt(kv[base + p, g, 1], do)
            pn = s_scr[p] * inv
            ds = (pn * (dp - delta)).astype(BF16)
            ds_scr[p * tok : (p + 1) * tok] = ds
            acc_v[g, p] += dot_nn(pn.astype(BF16), do)
            acc_k[g, p] += dot_nn(ds, q)
        dq_t = dot_nn(kt[g], ds_scr[...]) * scale
        blocks[1, :, :, lanes] = dq_t.T.astype(BF16).reshape(bpd, BLK, D)

    def block_copy(ch, o):
        target = lax.rem(me + o, n)
        return pltpu.make_async_remote_copy(
            src_ref=send.at[ch, target],
            dst_ref=recv[ch].at[me],
            send_sem=a_ssem.at[ch],
            recv_sem=a_rsem.at[ch],
            device_id={"ctx": target},
            device_id_type=pl.DeviceIdType.MESH,
        )

    def chunk_step(ch, carry):
        g = ch // chunks_group
        first = lax.rem(ch, chunks_group) == 0
        last = lax.rem(ch, chunks_group) == chunks_group - 1

        @pl.when(first)
        def _():
            stage_last(g)
            for d in range(pieces):
                kt[g, :, d * tok : (d + 1) * tok] = kv[base + d, g, 0].astype(F32).T.astype(BF16)
                vt[g, :, d * tok : (d + 1) * tok] = kv[base + d, g, 1].astype(F32).T.astype(BF16)

        def one_head(j, inner):
            head_step(ch, g, j)
            return inner

        lax.fori_loop(0, CHUNK, one_head, 0)

        for t in range(n):
            for c in range(CAP):
                b = tab_s[0, t * CAP + c]
                send[ch, t, c, 0] = blocks[0, b]
                send[ch, t, c, 1] = blocks[1, b]
        for cc in range(chunks):

            @pl.when(ch == cc)
            def _(cc=cc):
                recv[cc][me] = send[cc, me]
                for o in range(1, n):
                    block_copy(cc, o).start()

        for g2 in range(1, groups):

            @pl.when(ch == (g2 - 1) * chunks_group)
            def _(g2=g2):
                stage_two(g2)

            @pl.when(ch == (g2 - 1) * chunks_group + 1)
            def _(g2=g2):
                stage_three(g2)

            for k, stage in enumerate((reduce_two, reduce_three, reduce_four)):

                @pl.when(ch == g2 * chunks_group + k)
                def _(g2=g2, stage=stage):
                    stage(g2 - 1)

        @pl.when(last)
        def _():
            reduce_one(g)

        return carry

    lax.fori_loop(0, chunks, chunk_step, 0)

    def unpack(ch):
        held = recv[ch].at[pl.ds(0, n - 1)]
        pltpu.make_async_copy(held, held, a_rsem.at[ch]).wait()
        for slot in range(bpd):
            w = tab_s[1, slot]
            rows = slice(slot * BLK, (slot + 1) * BLK)
            cols = slice(ch * CHUNK * D, (ch + 1) * CHUNK * D)
            out_ref[rows, cols] = recv[ch][w // CAP, w % CAP, 0]
            dq_ref[rows, cols] = recv[ch][w // CAP, w % CAP, 1]

    reduce_two(groups - 1)
    for ch in range(chunks // 2):
        unpack(ch)
    reduce_three(groups - 1)
    for g in range(groups - 1):
        reduce_last(g)
    reduce_four(groups - 1)
    for ch in range(chunks // 2, chunks):
        unpack(ch)
    reduce_last(groups - 1)

    for ch in range(chunks):
        sent = send.at[ch, pl.ds(0, n - 1)]
        pltpu.make_async_copy(sent, sent, a_ssem.at[ch]).wait()
    for g in range(groups):
        stage_sent(g)
        reduce_sent(g)


def shards(q, k, v, do, lens, dest):
    n = lax.axis_size("ctx")
    tok, width = q.shape
    heads = width // D
    groups = k.shape[1] // D
    bpd = tok // BLK
    pieces = min(n, (MAX_DOC - 1 + tok - 1) // tok + 1)
    chunks = heads // CHUNK
    keys = pieces * tok
    smem = pl.BlockSpec(memory_space=pltpu.SMEM)
    vmem = pl.BlockSpec(memory_space=pltpu.VMEM)
    return pl.pallas_call(
        functools.partial(main_kernel, n, pieces),
        out_shape=(
            jax.ShapeDtypeStruct(q.shape, BF16),
            jax.ShapeDtypeStruct(q.shape, BF16),
            jax.ShapeDtypeStruct(k.shape, BF16),
            jax.ShapeDtypeStruct(v.shape, BF16),
        ),
        in_specs=[smem, vmem, vmem, vmem, vmem, vmem],
        out_specs=(vmem, vmem, vmem, vmem),
        scratch_shapes=[
            pltpu.VMEM((4 * ROW - 1, groups, 2, tok, D), BF16),
            pltpu.VMEM((groups, D, keys), BF16),
            pltpu.VMEM((groups, D, keys), BF16),
            pltpu.VMEM((pieces, tok, tok), F32),
            pltpu.VMEM((pieces, tok, tok), F32),
            pltpu.VMEM((keys, tok), BF16),
            pltpu.VMEM((keys, tok), BF16),
            pltpu.VMEM((groups, pieces, tok, D), F32),
            pltpu.VMEM((groups, pieces, tok, D), F32),
            pltpu.VMEM((2, bpd, BLK, CHUNK * D), BF16),
            pltpu.VMEM((chunks, n, CAP, 2, BLK, CHUNK * D), BF16),
            pltpu.VMEM((3 * ROW, groups, 2, tok, D), BF16),
            pltpu.VMEM((3 * ROW, groups, 2, tok, D), BF16),
            pltpu.SemaphoreType.DMA((3 * ROW, groups)),
            pltpu.SemaphoreType.DMA((4 * ROW - 1, groups)),
            pltpu.SemaphoreType.DMA((3 * ROW, groups)),
            pltpu.SemaphoreType.DMA((3 * ROW, groups)),
            pltpu.SemaphoreType.DMA((chunks,)),
            pltpu.SemaphoreType.DMA((chunks,)),
            pltpu.VMEM((2, n * bpd), jnp.int32),
            pltpu.SMEM((2, n * bpd), jnp.int32),
            pltpu.SemaphoreType.DMA(()),
        ]
        + [pltpu.VMEM((n, CAP, 2, BLK, CHUNK * D), BF16)] * chunks,
        compiler_params=pltpu.CompilerParams(
            collective_id=0, has_side_effects=True, vmem_limit_bytes=60 * 2**20
        ),
    )(lens, dest.reshape(1, n * bpd), q, do, k, v)


def solution(mesh):
    rows = P(("dp", "ctx"), "head")
    return jax.shard_map(
        shards,
        mesh=mesh,
        in_specs=(rows, rows, rows, rows, P("dp"), P("dp")),
        out_specs=(rows, rows, rows, rows),
        check_vma=False,
    )
```

```python
import functools
import math

import jax
import jax.numpy as jnp
from jax import lax
from jax.experimental import pallas as pl
from jax.experimental.pallas import tpu as pltpu
from jax.sharding import PartitionSpec as P

D = 128
BLK = 16
MAX_DOC = 2304
CAP = 2
CHUNK = 2
ROW = 4
F32 = jnp.float32
BF16 = jnp.bfloat16


def dot_nt(a, b):
    return lax.dot_general(a, b, (((1,), (1,)), ((), ())), preferred_element_type=F32)


def dot_nn(a, b):
    return lax.dot_general(a, b, (((1,), (0,)), ((), ())), preferred_element_type=F32)


def main_kernel(
    n,
    pieces,
    lens_ref,
    dest_ref,
    q_ref,
    do_ref,
    k_ref,
    v_ref,
    out_ref,
    dq_ref,
    dk_ref,
    dv_ref,
    kv,
    kt,
    vt,
    bias,
    s_scr,
    p_scr,
    ds_scr,
    acc_k,
    acc_v,
    blocks,
    send,
    g_send,
    g_recv,
    kv_ssem,
    kv_rsem,
    g_ssem,
    g_rsem,
    a_ssem,
    a_rsem,
    tab_v,
    tab_s,
    tab_sem,
    *recv,
):
    me = lax.axis_index("ctx")
    tok, width = q_ref.shape
    heads = width // D
    groups = k_ref.shape[1] // D
    per_group = heads // groups
    chunks = heads // CHUNK
    chunks_group = chunks // groups
    bpd = tok // BLK
    scale = 1.0 / math.sqrt(D)
    log2e_scale = scale * math.log2(math.e)

    barrier = pltpu.get_barrier_semaphore()
    for o in range(1, n):
        pl.semaphore_signal(
            barrier,
            inc=1,
            device_id={"ctx": lax.rem(me + o, n)},
            device_id_type=pl.DeviceIdType.MESH,
        )

    x, y = me // ROW, lax.rem(me, ROW)
    opp = lax.rem(y + ROW // 2, ROW)
    n_rows = n // ROW
    base = ROW - 1
    for g in range(groups):
        kv[base, g, 0] = k_ref[:, g * D : (g + 1) * D]
        kv[base, g, 1] = v_ref[:, g * D : (g + 1) * D]
    for d in range(1, pieces):

        @pl.when(me < d)
        def _(d=d):
            kv[base + d] = jnp.zeros_like(kv[base + d])

    pl.semaphore_wait(barrier, n - 1)

    def hop(g, message, src, dst, dx, ty, go):
        @pl.when(go)
        def _():
            pltpu.make_async_remote_copy(
                src_ref=kv.at[base + src, g],
                dst_ref=kv.at[base + dst, g],
                send_sem=kv_ssem.at[message, g],
                recv_sem=kv_rsem.at[base + dst, g],
                device_id={"ctx": (x + dx) * ROW + ty},
                device_id_type=pl.DeviceIdType.MESH,
            ).start()

    def drain(g, message, go):
        @pl.when(go)
        def _():
            held = kv.at[base, g]
            pltpu.make_async_copy(held, held, kv_ssem.at[message, g]).wait()

    def arrive(g, d, go):
        @pl.when(go)
        def _():
            held = kv.at[base + d, g]
            pltpu.make_async_copy(held, held, kv_rsem.at[base + d, g]).wait()

    def beside(k):
        return lax.rem(y + k, ROW)

    below = x < n_rows - 1
    third = (y == ROW - 1) & (x + 3 < n_rows)
    row_go = {k: (beside(k) > y) | (below if k == ROW // 2 else (y < 0)) for k in range(1, ROW)}
    far_opp = (x >= 1) & below & (2 * ROW + y - opp < pieces)
    far_go = {k: (x >= 2) & (2 * ROW + beside(k) - y < pieces) for k in (1, ROW - 1)}

    def stage_one(g):
        hop(g, 0, 0, ROW, 1, y, below)
        for k in range(1, ROW):
            hop(g, k, 0, beside(k) - y, 0, beside(k), row_go[k])
        hop(g, ROW, 0, 3 * ROW - y, 3, 0, third)

    def stage_two(g):
        arrive(g, ROW, x >= 1)
        hop(g, 5, ROW, 2 * ROW, 1, y, (x >= 1) & below)
        hop(g, 6, ROW, ROW + beside(1) - y, 0, beside(1), x >= 1)
        hop(g, 7, ROW, ROW + beside(ROW - 1) - y, 0, beside(ROW - 1), x >= 1)
        arrive(g, y - opp, below | (y > opp))
        hop(g, 8, y - opp, ROW + y - opp, 1, y, below)

    def stage_three(g):
        arrive(g, 2 * ROW, x >= 2)
        hop(g, 9, 2 * ROW, 2 * ROW + beside(1) - y, 0, beside(1), far_go[1])
        hop(g, 10, 2 * ROW, 2 * ROW + beside(ROW - 1) - y, 0, beside(ROW - 1), far_go[ROW - 1])
        arrive(g, ROW + y - opp, x >= 1)
        hop(g, 11, ROW + y - opp, 2 * ROW + y - opp, 1, y, far_opp)

    def stage_last(g):
        for k in (1, ROW - 1):
            side = beside(k)
            arrive(g, y - side, side < y)
            arrive(g, ROW + y - side, x >= 1)
            arrive(g, 2 * ROW + y - side, (x >= 2) & (2 * ROW + y - side < pieces))
        arrive(g, 2 * ROW + y - opp, (x >= 2) & (2 * ROW + y - opp < pieces))
        arrive(g, 2 * ROW + 1, (x >= 3) & (y == 0))

    def stage_sent(g):
        drain(g, 0, below)
        for k in range(1, ROW):
            drain(g, k, row_go[k])
        drain(g, ROW, third)
        drain(g, 5, (x >= 1) & below)
        drain(g, 6, x >= 1)
        drain(g, 7, x >= 1)
        drain(g, 8, below)
        drain(g, 9, far_go[1])
        drain(g, 10, far_go[ROW - 1])
        drain(g, 11, far_opp)

    def put(g, message, d):
        g_send[message, g, 0] = acc_k[g, d].astype(BF16)
        g_send[message, g, 1] = acc_v[g, d].astype(BF16)

    def ship(g, message, dx, ty):
        pltpu.make_async_remote_copy(
            src_ref=g_send.at[message, g],
            dst_ref=g_recv.at[message, g],
            send_sem=g_ssem.at[message, g],
            recv_sem=g_rsem.at[message, g],
            device_id={"ctx": (x - dx) * ROW + ty},
            device_id_type=pl.DeviceIdType.MESH,
        ).start()

    def give(g, message, d, dx, ty, go):
        @pl.when(go)
        def _():
            put(g, message, d)
            ship(g, message, dx, ty)

    def landed(g, message):
        held = g_recv.at[message, g]
        pltpu.make_async_copy(held, held, g_rsem.at[message, g]).wait()

    def take(g, message, d, go):
        @pl.when(go)
        def _():
            landed(g, message)
            acc_k[g, d] += g_recv[message, g, 0].astype(F32)
            acc_v[g, d] += g_recv[message, g, 1].astype(F32)

    nxt, prv = beside(1), beside(ROW - 1)
    opp_go = below | (opp < y)
    gives = [
        (x >= 2) & (2 * ROW + y - nxt < pieces),
        (x >= 2) & (2 * ROW + y - prv < pieces),
        x >= 1,
        x >= 1,
        (x >= 2) & (2 * ROW + y - opp < pieces),
        nxt < y,
        prv < y,
        (x >= 3) & (y == 0),
        x >= 2,
        x >= 1,
        x >= 1,
        opp_go,
    ]

    def reduce_one(g):
        give(g, 0, 2 * ROW + y - nxt, 0, nxt, gives[0])
        give(g, 1, 2 * ROW + y - prv, 0, prv, gives[1])
        give(g, 4, 2 * ROW + y - opp, 1, y, gives[4])
        give(g, 7, 2 * ROW + 1, 3, ROW - 1, gives[7])
        give(g, 2, ROW + y - nxt, 0, nxt, gives[2])
        give(g, 3, ROW + y - prv, 0, prv, gives[3])
        give(g, 5, y - nxt, 0, nxt, gives[5])
        give(g, 6, y - prv, 0, prv, gives[6])

    def reduce_two(g):
        take(g, 0, 2 * ROW, (x >= 2) & (2 * ROW + prv - y < pieces))
        take(g, 1, 2 * ROW, (x >= 2) & (2 * ROW + nxt - y < pieces))
        give(g, 8, 2 * ROW, 1, y, gives[8])

    def reduce_three(g):
        take(g, 4, ROW + y - opp, (x >= 1) & below & (2 * ROW + y - opp < pieces))
        give(g, 10, ROW + y - opp, 1, y, gives[10])
        take(g, 2, ROW, x >= 1)
        take(g, 3, ROW, x >= 1)
        take(g, 8, ROW, (x >= 1) & below)
        give(g, 9, ROW, 1, y, gives[9])

    def reduce_four(g):
        @pl.when(opp < y)
        def _():
            @pl.when(below)
            def _():
                landed(g, 10)
                acc_k[g, y - opp] += g_recv[10, g, 0].astype(F32)
                acc_v[g, y - opp] += g_recv[10, g, 1].astype(F32)

            put(g, 11, y - opp)

        @pl.when((opp > y) & below)
        def _():
            landed(g, 10)
            g_send[11, g] = g_recv[10, g]

        @pl.when(opp_go)
        def _():
            ship(g, 11, 0, opp)

    def reduce_last(g):
        take(g, 5, 0, y < prv)
        take(g, 6, 0, y < nxt)
        take(g, 7, 0, (y == ROW - 1) & (x + 3 < n_rows))
        take(g, 9, 0, below)
        take(g, 11, 0, below | (y < opp))
        dk_ref[:, g * D : (g + 1) * D] = (acc_k[g, 0] * scale).astype(BF16)
        dv_ref[:, g * D : (g + 1) * D] = acc_v[g, 0].astype(BF16)

    def reduce_sent(g):
        for message, go in enumerate(gives):

            @pl.when(go)
            def _(message=message):
                held = g_send.at[message, g]
                pltpu.make_async_copy(held, held, g_ssem.at[message, g]).wait()

    stage_one(0)

    nb = n * bpd
    lane = lax.broadcasted_iota(jnp.int32, (nb, nb), 1)
    sub = lax.broadcasted_iota(jnp.int32, (nb, nb), 0)
    dest_row = jnp.broadcast_to(dest_ref[...], (nb, nb))
    dest_col = dest_row.T
    same = (dest_row // bpd == dest_col // bpd) & (lane // bpd == sub // bpd) & (lane < sub)
    rank = jnp.sum(jnp.where(same, 1.0, 0.0).astype(F32), axis=1, keepdims=True).astype(jnp.int32)
    slot = (dest_col // bpd) * CAP + rank
    picked = (sub // bpd == me) & (slot == lane)
    src_row = jnp.sum(jnp.where(picked, sub - me * bpd, 0), axis=0, keepdims=True)
    tab_v[0:1] = jnp.clip(src_row, 0, bpd - 1)
    found = dest_col == me * bpd + lane
    want_row = jnp.sum(jnp.where(found, (sub // bpd) * CAP + rank, 0), axis=0, keepdims=True)
    tab_v[1:2] = jnp.clip(want_row, 0, n * CAP - 1)
    to_smem = pltpu.make_async_copy(tab_v, tab_s, tab_sem)
    to_smem.start()

    acc_k[...] = jnp.zeros_like(acc_k)
    acc_v[...] = jnp.zeros_like(acc_v)
    query_pos = me * tok + lax.broadcasted_iota(jnp.int32, (1, tok), 1)
    end = jnp.int32(0)
    start = jnp.zeros((1, tok), jnp.int32)
    for doc in range(lens_ref.shape[0]):
        end = end + lens_ref[doc]
        start = start + jnp.where(end <= query_pos, lens_ref[doc], 0)
    for p in range(pieces):
        key_pos = (me - p) * tok + lax.broadcasted_iota(jnp.int32, (tok, tok), 0)
        seen = (key_pos >= start) & (key_pos <= query_pos)
        bias[p] = jnp.where(seen, 0.0, -jnp.inf).astype(F32)

    to_smem.wait()
    stage_two(0)
    stage_three(0)
    for g in range(1, groups):
        stage_one(g)

    def fold(x, op):
        return op(x.reshape(tok // 8, 8, tok), axis=0)

    def pair_step(ch, g):
        cols = [pl.ds(pl.multiple_of((ch * CHUNK + j) * D, D), D) for j in range(CHUNK)]
        qs = [q_ref[:, c] for c in cols]
        dos = [do_ref[:, c] for c in cols]
        peaks, totals = [None] * CHUNK, [None] * CHUNK

        def score(j, p):
            s = dot_nt(kv[base + p, g, 0], qs[j]) + bias[p]
            s_scr[j, p] = s
            top = fold(s, jnp.max)
            peaks[j] = top if p == 0 else jnp.maximum(peaks[j], top)

        def weigh(j, p):
            e = jnp.exp2((s_scr[j, p] - peaks[j]) * log2e_scale)
            s_scr[j, p] = e
            p_scr[j, p * tok : (p + 1) * tok] = e.astype(BF16)
            part = fold(e, jnp.sum)
            totals[j] = part if p == 0 else totals[j] + part

        invs, deltas = [None] * CHUNK, [None] * CHUNK

        def attend(j):
            invs[j] = 1.0 / jnp.sum(totals[j], axis=0, keepdims=True)
            out_t = (dot_nn(vt[g], p_scr[j]) * invs[j]).astype(BF16).astype(F32)
            deltas[j] = jnp.sum(out_t * dos[j].astype(F32).T, axis=0, keepdims=True)
            blocks[0, :, :, j * D : (j + 1) * D] = out_t.T.astype(BF16).reshape(bpd, BLK, D)

        for j in range(CHUNK):
            for p in range(pieces):
                score(j, p)
                if j > 0:
                    weigh(j - 1, p)
            peaks[j] = jnp.max(peaks[j], axis=0, keepdims=True)
            if j > 0:
                attend(j - 1)
        for p in range(pieces):
            weigh(CHUNK - 1, p)
        attend(CHUNK - 1)
        do_cat = jnp.concatenate(dos, axis=0)
        q_cat = jnp.concatenate(qs, axis=0)
        for p in range(pieces):
            pns, dss = [], []
            for j in range(CHUNK):
                dp = dot_nt(kv[base + p, g, 1], dos[j])
                pn = s_scr[j, p] * invs[j]
                ds = (pn * (dp - deltas[j])).astype(BF16)
                ds_scr[j, p * tok : (p + 1) * tok] = ds
                dss.append(ds)
                pns.append(pn.astype(BF16))
            acc_v[g, p] += dot_nn(jnp.concatenate(pns, axis=1), do_cat)
            acc_k[g, p] += dot_nn(jnp.concatenate(dss, axis=1), q_cat)
        for j in range(CHUNK):
            dq_t = dot_nn(kt[g], ds_scr[j]) * scale
            blocks[1, :, :, j * D : (j + 1) * D] = dq_t.T.astype(BF16).reshape(bpd, BLK, D)

    def block_copy(ch, o):
        target = lax.rem(me + o, n)
        return pltpu.make_async_remote_copy(
            src_ref=send.at[ch, target],
            dst_ref=recv[ch].at[me],
            send_sem=a_ssem.at[ch],
            recv_sem=a_rsem.at[ch],
            device_id={"ctx": target},
            device_id_type=pl.DeviceIdType.MESH,
        )

    def chunk_step(ch, carry):
        g = ch // chunks_group
        first = lax.rem(ch, chunks_group) == 0
        last = lax.rem(ch, chunks_group) == chunks_group - 1

        @pl.when(first)
        def _():
            stage_last(g)
            for d in range(pieces):
                kt[g, :, d * tok : (d + 1) * tok] = kv[base + d, g, 0].astype(F32).T.astype(BF16)
                vt[g, :, d * tok : (d + 1) * tok] = kv[base + d, g, 1].astype(F32).T.astype(BF16)

        pair_step(ch, g)

        @pl.when(last)
        def _():
            reduce_one(g)

        for t in range(n):
            for c in range(CAP):
                b = tab_s[0, t * CAP + c]
                send[ch, t, c, 0] = blocks[0, b]
                send[ch, t, c, 1] = blocks[1, b]
        for cc in range(chunks):

            @pl.when(ch == cc)
            def _(cc=cc):
                recv[cc][me] = send[cc, me]
                for o in range(1, n):
                    block_copy(cc, o).start()

        for g2 in range(1, groups):

            @pl.when(ch == (g2 - 1) * chunks_group)
            def _(g2=g2):
                stage_two(g2)

            @pl.when(ch == (g2 - 1) * chunks_group + 1)
            def _(g2=g2):
                stage_three(g2)

            for k, stage in enumerate((reduce_two, reduce_three, reduce_four)):

                @pl.when(ch == g2 * chunks_group + k + 1)
                def _(g2=g2, stage=stage):
                    stage(g2 - 1)

        return carry

    lax.fori_loop(0, chunks, chunk_step, 0)

    def unpack(ch):
        held = recv[ch].at[pl.ds(0, n - 1)]
        pltpu.make_async_copy(held, held, a_rsem.at[ch]).wait()
        for slot in range(bpd):
            w = tab_s[1, slot]
            rows = slice(slot * BLK, (slot + 1) * BLK)
            cols = slice(ch * CHUNK * D, (ch + 1) * CHUNK * D)
            out_ref[rows, cols] = recv[ch][w // CAP, w % CAP, 0]
            dq_ref[rows, cols] = recv[ch][w // CAP, w % CAP, 1]

    reduce_two(groups - 1)
    reduce_three(groups - 1)
    for g in range(groups - 1):
        reduce_last(g)
    reduce_four(groups - 1)
    for ch in range(chunks):
        unpack(ch)
    reduce_last(groups - 1)

    for ch in range(chunks):
        sent = send.at[ch, pl.ds(0, n - 1)]
        pltpu.make_async_copy(sent, sent, a_ssem.at[ch]).wait()
    for g in range(groups):
        stage_sent(g)
        reduce_sent(g)


def shards(q, k, v, do, lens, dest):
    n = lax.axis_size("ctx")
    tok, width = q.shape
    heads = width // D
    groups = k.shape[1] // D
    bpd = tok // BLK
    pieces = min(n, (MAX_DOC - 1 + tok - 1) // tok + 1)
    chunks = heads // CHUNK
    keys = pieces * tok
    smem = pl.BlockSpec(memory_space=pltpu.SMEM)
    vmem = pl.BlockSpec(memory_space=pltpu.VMEM)
    return pl.pallas_call(
        functools.partial(main_kernel, n, pieces),
        out_shape=(
            jax.ShapeDtypeStruct(q.shape, BF16),
            jax.ShapeDtypeStruct(q.shape, BF16),
            jax.ShapeDtypeStruct(k.shape, BF16),
            jax.ShapeDtypeStruct(v.shape, BF16),
        ),
        in_specs=[smem, vmem, vmem, vmem, vmem, vmem],
        out_specs=(vmem, vmem, vmem, vmem),
        scratch_shapes=[
            pltpu.VMEM((4 * ROW - 1, groups, 2, tok, D), BF16),
            pltpu.VMEM((groups, D, keys), BF16),
            pltpu.VMEM((groups, D, keys), BF16),
            pltpu.VMEM((pieces, tok, tok), F32),
            pltpu.VMEM((CHUNK, pieces, tok, tok), F32),
            pltpu.VMEM((CHUNK, keys, tok), BF16),
            pltpu.VMEM((CHUNK, keys, tok), BF16),
            pltpu.VMEM((groups, pieces, tok, D), F32),
            pltpu.VMEM((groups, pieces, tok, D), F32),
            pltpu.VMEM((2, bpd, BLK, CHUNK * D), BF16),
            pltpu.VMEM((chunks, n, CAP, 2, BLK, CHUNK * D), BF16),
            pltpu.VMEM((3 * ROW, groups, 2, tok, D), BF16),
            pltpu.VMEM((3 * ROW, groups, 2, tok, D), BF16),
            pltpu.SemaphoreType.DMA((3 * ROW, groups)),
            pltpu.SemaphoreType.DMA((4 * ROW - 1, groups)),
            pltpu.SemaphoreType.DMA((3 * ROW, groups)),
            pltpu.SemaphoreType.DMA((3 * ROW, groups)),
            pltpu.SemaphoreType.DMA((chunks,)),
            pltpu.SemaphoreType.DMA((chunks,)),
            pltpu.VMEM((2, n * bpd), jnp.int32),
            pltpu.SMEM((2, n * bpd), jnp.int32),
            pltpu.SemaphoreType.DMA(()),
        ]
        + [pltpu.VMEM((n, CAP, 2, BLK, CHUNK * D), BF16)] * chunks,
        compiler_params=pltpu.CompilerParams(
            collective_id=0, has_side_effects=True, vmem_limit_bytes=60 * 2**20
        ),
    )(lens, dest.reshape(1, n * bpd), q, do, k, v)


def solution(mesh):
    rows = P(("dp", "ctx"), "head")
    return jax.shard_map(
        shards,
        mesh=mesh,
        in_specs=(rows, rows, rows, rows, P("dp"), P("dp")),
        out_specs=(rows, rows, rows, rows),
        check_vma=False,
    )
```

```python
import functools
import math

import jax
import jax.numpy as jnp
from jax import lax
from jax.experimental import pallas as pl
from jax.experimental.pallas import tpu as pltpu
from jax.sharding import PartitionSpec as P

D = 128
BLK = 16
MAX_DOC = 2304
CAP = 2
CHUNK = 2
ROW = 4
F32 = jnp.float32
BF16 = jnp.bfloat16


def dot_nt(a, b):
    return lax.dot_general(a, b, (((1,), (1,)), ((), ())), preferred_element_type=F32)


def dot_nn(a, b):
    return lax.dot_general(a, b, (((1,), (0,)), ((), ())), preferred_element_type=F32)


def main_kernel(
    n,
    pieces,
    lens_ref,
    dest_ref,
    q_ref,
    do_ref,
    k_ref,
    v_ref,
    recv,
    tab_v,
    dk_ref,
    dv_ref,
    kv,
    kt,
    vt,
    bias,
    s_scr,
    p_scr,
    ds_scr,
    acc_k,
    acc_v,
    blocks,
    send,
    g_send,
    g_recv,
    kv_ssem,
    kv_rsem,
    g_ssem,
    g_rsem,
    a_ssem,
    a_rsem,
    tab_s,
    tab_sem,
    own_sem,
):
    me = lax.axis_index("ctx")
    tok, width = q_ref.shape
    heads = width // D
    groups = k_ref.shape[1] // D
    per_group = heads // groups
    chunks = heads // CHUNK
    chunks_group = chunks // groups
    bpd = tok // BLK
    scale = 1.0 / math.sqrt(D)
    log2e_scale = scale * math.log2(math.e)

    barrier = pltpu.get_barrier_semaphore()
    for o in range(1, n):
        pl.semaphore_signal(
            barrier,
            inc=1,
            device_id={"ctx": lax.rem(me + o, n)},
            device_id_type=pl.DeviceIdType.MESH,
        )

    x, y = me // ROW, lax.rem(me, ROW)
    opp = lax.rem(y + ROW // 2, ROW)
    n_rows = n // ROW
    base = ROW - 1
    for g in range(groups):
        kv[base, g, 0] = k_ref[:, g * D : (g + 1) * D]
        kv[base, g, 1] = v_ref[:, g * D : (g + 1) * D]
    for d in range(1, pieces):

        @pl.when(me < d)
        def _(d=d):
            kv[base + d] = jnp.zeros_like(kv[base + d])

    pl.semaphore_wait(barrier, n - 1)

    def hop(g, message, src, dst, dx, ty, go):
        @pl.when(go)
        def _():
            pltpu.make_async_remote_copy(
                src_ref=kv.at[base + src, g],
                dst_ref=kv.at[base + dst, g],
                send_sem=kv_ssem.at[message, g],
                recv_sem=kv_rsem.at[base + dst, g],
                device_id={"ctx": (x + dx) * ROW + ty},
                device_id_type=pl.DeviceIdType.MESH,
            ).start()

    def drain(g, message, go):
        @pl.when(go)
        def _():
            held = kv.at[base, g]
            pltpu.make_async_copy(held, held, kv_ssem.at[message, g]).wait()

    def arrive(g, d, go):
        @pl.when(go)
        def _():
            held = kv.at[base + d, g]
            pltpu.make_async_copy(held, held, kv_rsem.at[base + d, g]).wait()

    def beside(k):
        return lax.rem(y + k, ROW)

    below = x < n_rows - 1
    third = (y == ROW - 1) & (x + 3 < n_rows)
    row_go = {k: (beside(k) > y) | (below if k == ROW // 2 else (y < 0)) for k in range(1, ROW)}
    far_opp = (x >= 1) & below & (2 * ROW + y - opp < pieces)
    far_go = {k: (x >= 2) & (2 * ROW + beside(k) - y < pieces) for k in (1, ROW - 1)}

    def stage_one(g):
        hop(g, 0, 0, ROW, 1, y, below)
        for k in range(1, ROW):
            hop(g, k, 0, beside(k) - y, 0, beside(k), row_go[k])
        hop(g, ROW, 0, 3 * ROW - y, 3, 0, third)

    def stage_two(g):
        arrive(g, ROW, x >= 1)
        hop(g, 5, ROW, 2 * ROW, 1, y, (x >= 1) & below)
        hop(g, 6, ROW, ROW + beside(1) - y, 0, beside(1), x >= 1)
        hop(g, 7, ROW, ROW + beside(ROW - 1) - y, 0, beside(ROW - 1), x >= 1)
        arrive(g, y - opp, below | (y > opp))
        hop(g, 8, y - opp, ROW + y - opp, 1, y, below)

    def stage_three(g):
        arrive(g, 2 * ROW, x >= 2)
        hop(g, 9, 2 * ROW, 2 * ROW + beside(1) - y, 0, beside(1), far_go[1])
        hop(g, 10, 2 * ROW, 2 * ROW + beside(ROW - 1) - y, 0, beside(ROW - 1), far_go[ROW - 1])
        arrive(g, ROW + y - opp, x >= 1)
        hop(g, 11, ROW + y - opp, 2 * ROW + y - opp, 1, y, far_opp)

    def stage_last(g):
        for k in (1, ROW - 1):
            side = beside(k)
            arrive(g, y - side, side < y)
            arrive(g, ROW + y - side, x >= 1)
            arrive(g, 2 * ROW + y - side, (x >= 2) & (2 * ROW + y - side < pieces))
        arrive(g, 2 * ROW + y - opp, (x >= 2) & (2 * ROW + y - opp < pieces))
        arrive(g, 2 * ROW + 1, (x >= 3) & (y == 0))

    def stage_sent(g):
        drain(g, 0, below)
        for k in range(1, ROW):
            drain(g, k, row_go[k])
        drain(g, ROW, third)
        drain(g, 5, (x >= 1) & below)
        drain(g, 6, x >= 1)
        drain(g, 7, x >= 1)
        drain(g, 8, below)
        drain(g, 9, far_go[1])
        drain(g, 10, far_go[ROW - 1])
        drain(g, 11, far_opp)

    def put(g, message, d):
        g_send[message, g, 0] = acc_k[g, d].astype(BF16)
        g_send[message, g, 1] = acc_v[g, d].astype(BF16)

    def ship(g, message, dx, ty):
        pltpu.make_async_remote_copy(
            src_ref=g_send.at[message, g],
            dst_ref=g_recv.at[message, g],
            send_sem=g_ssem.at[message, g],
            recv_sem=g_rsem.at[message, g],
            device_id={"ctx": (x - dx) * ROW + ty},
            device_id_type=pl.DeviceIdType.MESH,
        ).start()

    def give(g, message, d, dx, ty, go):
        @pl.when(go)
        def _():
            put(g, message, d)
            ship(g, message, dx, ty)

    def landed(g, message):
        held = g_recv.at[message, g]
        pltpu.make_async_copy(held, held, g_rsem.at[message, g]).wait()

    def take(g, message, d, go):
        @pl.when(go)
        def _():
            landed(g, message)
            acc_k[g, d] += g_recv[message, g, 0].astype(F32)
            acc_v[g, d] += g_recv[message, g, 1].astype(F32)

    nxt, prv = beside(1), beside(ROW - 1)
    opp_go = below | (opp < y)
    gives = [
        (x >= 2) & (2 * ROW + y - nxt < pieces),
        (x >= 2) & (2 * ROW + y - prv < pieces),
        x >= 1,
        x >= 1,
        (x >= 2) & (2 * ROW + y - opp < pieces),
        nxt < y,
        prv < y,
        (x >= 3) & (y == 0),
        x >= 2,
        x >= 1,
        x >= 1,
        opp_go,
    ]

    def reduce_one(g):
        give(g, 0, 2 * ROW + y - nxt, 0, nxt, gives[0])
        give(g, 1, 2 * ROW + y - prv, 0, prv, gives[1])
        give(g, 4, 2 * ROW + y - opp, 1, y, gives[4])
        give(g, 7, 2 * ROW + 1, 3, ROW - 1, gives[7])
        give(g, 2, ROW + y - nxt, 0, nxt, gives[2])
        give(g, 3, ROW + y - prv, 0, prv, gives[3])
        give(g, 5, y - nxt, 0, nxt, gives[5])
        give(g, 6, y - prv, 0, prv, gives[6])

    def reduce_two(g):
        take(g, 0, 2 * ROW, (x >= 2) & (2 * ROW + prv - y < pieces))
        take(g, 1, 2 * ROW, (x >= 2) & (2 * ROW + nxt - y < pieces))
        give(g, 8, 2 * ROW, 1, y, gives[8])

    def reduce_three(g):
        take(g, 4, ROW + y - opp, (x >= 1) & below & (2 * ROW + y - opp < pieces))
        give(g, 10, ROW + y - opp, 1, y, gives[10])
        take(g, 2, ROW, x >= 1)
        take(g, 3, ROW, x >= 1)
        take(g, 8, ROW, (x >= 1) & below)
        give(g, 9, ROW, 1, y, gives[9])

    def reduce_four(g):
        @pl.when(opp < y)
        def _():
            @pl.when(below)
            def _():
                landed(g, 10)
                acc_k[g, y - opp] += g_recv[10, g, 0].astype(F32)
                acc_v[g, y - opp] += g_recv[10, g, 1].astype(F32)

            put(g, 11, y - opp)

        @pl.when((opp > y) & below)
        def _():
            landed(g, 10)
            g_send[11, g] = g_recv[10, g]

        @pl.when(opp_go)
        def _():
            ship(g, 11, 0, opp)

    def reduce_last(g):
        take(g, 5, 0, y < prv)
        take(g, 6, 0, y < nxt)
        take(g, 7, 0, (y == ROW - 1) & (x + 3 < n_rows))
        take(g, 9, 0, below)
        take(g, 11, 0, below | (y < opp))
        dk_ref[:, g * D : (g + 1) * D] = (acc_k[g, 0] * scale).astype(BF16)
        dv_ref[:, g * D : (g + 1) * D] = acc_v[g, 0].astype(BF16)

    def reduce_sent(g):
        for message, go in enumerate(gives):

            @pl.when(go)
            def _(message=message):
                held = g_send.at[message, g]
                pltpu.make_async_copy(held, held, g_ssem.at[message, g]).wait()

    stage_one(0)

    nb = n * bpd
    lane = lax.broadcasted_iota(jnp.int32, (nb, nb), 1)
    sub = lax.broadcasted_iota(jnp.int32, (nb, nb), 0)
    dest_row = jnp.broadcast_to(dest_ref[...], (nb, nb))
    dest_col = dest_row.T
    same = (dest_row // bpd == dest_col // bpd) & (lane // bpd == sub // bpd) & (lane < sub)
    rank = jnp.sum(jnp.where(same, 1.0, 0.0).astype(F32), axis=1, keepdims=True).astype(jnp.int32)
    slot = (dest_col // bpd) * CAP + rank
    picked = (sub // bpd == me) & (slot == lane)
    src_row = jnp.sum(jnp.where(picked, sub - me * bpd, 0), axis=0, keepdims=True)
    tab_v[0:1] = jnp.clip(src_row, 0, bpd - 1)
    found = dest_col == me * bpd + lane
    want_row = jnp.sum(jnp.where(found, (sub // bpd) * CAP + rank, 0), axis=0, keepdims=True)
    tab_v[1:2] = jnp.clip(want_row, 0, n * CAP - 1)
    to_smem = pltpu.make_async_copy(tab_v, tab_s, tab_sem)
    to_smem.start()

    acc_k[...] = jnp.zeros_like(acc_k)
    acc_v[...] = jnp.zeros_like(acc_v)
    query_pos = me * tok + lax.broadcasted_iota(jnp.int32, (1, tok), 1)
    end = jnp.int32(0)
    start = jnp.zeros((1, tok), jnp.int32)
    for doc in range(lens_ref.shape[0]):
        end = end + lens_ref[doc]
        start = start + jnp.where(end <= query_pos, lens_ref[doc], 0)
    for p in range(pieces):
        key_pos = (me - p) * tok + lax.broadcasted_iota(jnp.int32, (tok, tok), 0)
        seen = (key_pos >= start) & (key_pos <= query_pos)
        bias[p] = jnp.where(seen, 0.0, -jnp.inf).astype(F32)

    to_smem.wait()
    stage_two(0)
    stage_three(0)
    for g in range(1, groups):
        stage_one(g)

    def fold(x, op):
        return op(x.reshape(tok // 8, 8, tok), axis=0)

    def pair_step(ch, g):
        cols = [pl.ds(pl.multiple_of((ch * CHUNK + j) * D, D), D) for j in range(CHUNK)]
        qs = [q_ref[:, c] for c in cols]
        dos = [do_ref[:, c] for c in cols]
        peaks, totals = [None] * CHUNK, [None] * CHUNK

        def score(j, p):
            s = dot_nt(kv[base + p, g, 0], qs[j]) + bias[p]
            s_scr[j, p] = s
            top = fold(s, jnp.max)
            peaks[j] = top if p == 0 else jnp.maximum(peaks[j], top)

        def weigh(j, p):
            e = jnp.exp2((s_scr[j, p] - peaks[j]) * log2e_scale)
            s_scr[j, p] = e
            p_scr[j, p * tok : (p + 1) * tok] = e.astype(BF16)
            part = fold(e, jnp.sum)
            totals[j] = part if p == 0 else totals[j] + part

        invs, deltas = [None] * CHUNK, [None] * CHUNK

        def attend(j):
            invs[j] = 1.0 / jnp.sum(totals[j], axis=0, keepdims=True)
            out_t = (dot_nn(vt[g], p_scr[j]) * invs[j]).astype(BF16).astype(F32)
            deltas[j] = jnp.sum(out_t * dos[j].astype(F32).T, axis=0, keepdims=True)
            blocks[0, :, :, j * D : (j + 1) * D] = out_t.T.astype(BF16).reshape(bpd, BLK, D)

        for j in range(CHUNK):
            for p in range(pieces):
                score(j, p)
                if j > 0:
                    weigh(j - 1, p)
            peaks[j] = jnp.max(peaks[j], axis=0, keepdims=True)
            if j > 0:
                attend(j - 1)
        for p in range(pieces):
            weigh(CHUNK - 1, p)
        attend(CHUNK - 1)
        do_cat = jnp.concatenate(dos, axis=0)
        q_cat = jnp.concatenate(qs, axis=0)
        for p in range(pieces):
            pns, dss = [], []
            for j in range(CHUNK):
                dp = dot_nt(kv[base + p, g, 1], dos[j])
                pn = s_scr[j, p] * invs[j]
                ds = (pn * (dp - deltas[j])).astype(BF16)
                ds_scr[j, p * tok : (p + 1) * tok] = ds
                dss.append(ds)
                pns.append(pn.astype(BF16))
            acc_v[g, p] += dot_nn(jnp.concatenate(pns, axis=1), do_cat)
            acc_k[g, p] += dot_nn(jnp.concatenate(dss, axis=1), q_cat)
        for j in range(CHUNK):
            dq_t = dot_nn(kt[g], ds_scr[j]) * scale
            blocks[1, :, :, j * D : (j + 1) * D] = dq_t.T.astype(BF16).reshape(bpd, BLK, D)

    def lanes(ch):
        return pl.ds(pl.multiple_of(ch * CHUNK * D, CHUNK * D), CHUNK * D)

    def block_copy(ch, o):
        target = lax.rem(me + o, n)
        return pltpu.make_async_remote_copy(
            src_ref=send.at[ch, target],
            dst_ref=recv.at[me, :, :, :, lanes(ch)],
            send_sem=a_ssem.at[ch],
            recv_sem=a_rsem.at[ch],
            device_id={"ctx": target},
            device_id_type=pl.DeviceIdType.MESH,
        )

    def own_copy(ch):
        return pltpu.make_async_copy(
            send.at[ch, me], recv.at[me, :, :, :, lanes(ch)], own_sem.at[ch]
        )

    def chunk_step(ch, carry):
        g = ch // chunks_group
        first = lax.rem(ch, chunks_group) == 0
        last = lax.rem(ch, chunks_group) == chunks_group - 1

        @pl.when(first)
        def _():
            stage_last(g)
            for d in range(pieces):
                kt[g, :, d * tok : (d + 1) * tok] = kv[base + d, g, 0].astype(F32).T.astype(BF16)
                vt[g, :, d * tok : (d + 1) * tok] = kv[base + d, g, 1].astype(F32).T.astype(BF16)

        pair_step(ch, g)

        @pl.when(last)
        def _():
            reduce_one(g)

        for t in range(n):
            for c in range(CAP):
                b = tab_s[0, t * CAP + c]
                send[ch, t, c, 0] = blocks[0, b]
                send[ch, t, c, 1] = blocks[1, b]
        for o in range(1, n):
            block_copy(ch, o).start()
        own_copy(ch).start()

        for g2 in range(1, groups):

            @pl.when(ch == (g2 - 1) * chunks_group)
            def _(g2=g2):
                stage_two(g2)

            @pl.when(ch == (g2 - 1) * chunks_group + 1)
            def _(g2=g2):
                stage_three(g2)

            for k, stage in enumerate((reduce_two, reduce_three, reduce_four)):

                @pl.when(ch == g2 * chunks_group + k + 1)
                def _(g2=g2, stage=stage):
                    stage(g2 - 1)

        return carry

    lax.fori_loop(0, chunks, chunk_step, 0)

    reduce_two(groups - 1)
    reduce_three(groups - 1)
    for g in range(groups - 1):
        reduce_last(g)
    reduce_four(groups - 1)
    reduce_last(groups - 1)

    for ch in range(chunks):
        own_copy(ch).wait()
        sent = send.at[ch, pl.ds(0, n - 1)]
        pltpu.make_async_copy(sent, sent, a_ssem.at[ch]).wait()
        held = recv.at[pl.ds(0, n - 1), :, :, :, lanes(ch)]
        pltpu.make_async_copy(held, held, a_rsem.at[ch]).wait()
    for g in range(groups):
        stage_sent(g)
        reduce_sent(g)


def place_kernel(
    tab_ref, recv, dk_in, dv_in, out_ref, dq_ref, dk_ref, dv_ref, held, kept, in_sem, out_sem
):
    bpd = out_ref.shape[0] // BLK
    moves = []
    for slot in range(bpd):
        w = tab_ref[1, slot]
        rows = pl.ds(slot * BLK, BLK)
        for i, ref in enumerate((out_ref, dq_ref)):
            moves.append((recv.at[w // CAP, w % CAP, i], held.at[i, slot], ref.at[rows]))
    for i, (source, ref) in enumerate(((dk_in, dk_ref), (dv_in, dv_ref))):
        moves.append((source, kept.at[i], ref))
    loads = [pltpu.make_async_copy(m[0], m[1], in_sem.at[i]) for i, m in enumerate(moves)]
    stores = [pltpu.make_async_copy(m[1], m[2], out_sem.at[i]) for i, m in enumerate(moves)]
    for load in loads:
        load.start()
    for load, store in zip(loads, stores):
        load.wait()
        store.start()
    for store in stores:
        store.wait()


def shards(q, k, v, do, lens, dest):
    n = lax.axis_size("ctx")
    tok, width = q.shape
    heads = width // D
    groups = k.shape[1] // D
    bpd = tok // BLK
    pieces = min(n, (MAX_DOC - 1 + tok - 1) // tok + 1)
    chunks = heads // CHUNK
    keys = pieces * tok
    smem = pl.BlockSpec(memory_space=pltpu.SMEM)
    vmem = pl.BlockSpec(memory_space=pltpu.VMEM)
    hbm = pl.BlockSpec(memory_space=pl.ANY)
    recv, tab, dk, dv = pl.pallas_call(
        functools.partial(main_kernel, n, pieces),
        out_shape=(
            jax.ShapeDtypeStruct((n, CAP, 2, BLK, width), BF16),
            jax.ShapeDtypeStruct((2, n * bpd), jnp.int32),
            jax.ShapeDtypeStruct(k.shape, BF16),
            jax.ShapeDtypeStruct(v.shape, BF16),
        ),
        in_specs=[smem, vmem, vmem, vmem, vmem, vmem],
        out_specs=(hbm, vmem, vmem, vmem),
        scratch_shapes=[
            pltpu.VMEM((4 * ROW - 1, groups, 2, tok, D), BF16),
            pltpu.VMEM((groups, D, keys), BF16),
            pltpu.VMEM((groups, D, keys), BF16),
            pltpu.VMEM((pieces, tok, tok), F32),
            pltpu.VMEM((CHUNK, pieces, tok, tok), F32),
            pltpu.VMEM((CHUNK, keys, tok), BF16),
            pltpu.VMEM((CHUNK, keys, tok), BF16),
            pltpu.VMEM((groups, pieces, tok, D), F32),
            pltpu.VMEM((groups, pieces, tok, D), F32),
            pltpu.VMEM((2, bpd, BLK, CHUNK * D), BF16),
            pltpu.VMEM((chunks, n, CAP, 2, BLK, CHUNK * D), BF16),
            pltpu.VMEM((3 * ROW, groups, 2, tok, D), BF16),
            pltpu.VMEM((3 * ROW, groups, 2, tok, D), BF16),
            pltpu.SemaphoreType.DMA((3 * ROW, groups)),
            pltpu.SemaphoreType.DMA((4 * ROW - 1, groups)),
            pltpu.SemaphoreType.DMA((3 * ROW, groups)),
            pltpu.SemaphoreType.DMA((3 * ROW, groups)),
            pltpu.SemaphoreType.DMA((chunks,)),
            pltpu.SemaphoreType.DMA((chunks,)),
            pltpu.SMEM((2, n * bpd), jnp.int32),
            pltpu.SemaphoreType.DMA(()),
            pltpu.SemaphoreType.DMA((chunks,)),
        ],
        compiler_params=pltpu.CompilerParams(
            collective_id=0, has_side_effects=True, vmem_limit_bytes=60 * 2**20
        ),
    )(lens, dest.reshape(1, n * bpd), q, do, k, v)
    return pl.pallas_call(
        place_kernel,
        out_shape=(
            jax.ShapeDtypeStruct(q.shape, BF16),
            jax.ShapeDtypeStruct(q.shape, BF16),
            jax.ShapeDtypeStruct(k.shape, BF16),
            jax.ShapeDtypeStruct(v.shape, BF16),
        ),
        in_specs=[smem, hbm, hbm, hbm],
        out_specs=(hbm, hbm, hbm, hbm),
        scratch_shapes=[
            pltpu.VMEM((2, bpd, BLK, width), BF16),
            pltpu.VMEM((2, *k.shape), BF16),
            pltpu.SemaphoreType.DMA((2 * bpd + 2,)),
            pltpu.SemaphoreType.DMA((2 * bpd + 2,)),
        ],
    )(tab, recv, dk, dv)


def solution(mesh):
    rows = P(("dp", "ctx"), "head")
    return jax.shard_map(
        shards,
        mesh=mesh,
        in_specs=(rows, rows, rows, rows, P("dp"), P("dp")),
        out_specs=(rows, rows, rows, rows),
        check_vma=False,
    )
```

```python
import functools
import math

import jax
import jax.numpy as jnp
from jax import lax
from jax.experimental import pallas as pl
from jax.experimental.pallas import tpu as pltpu
from jax.sharding import PartitionSpec as P

D = 128
BLK = 16
MAX_DOC = 2304
CAP = 2
CHUNK = 2
ROW = 4
F32 = jnp.float32
BF16 = jnp.bfloat16


def dot_nt(a, b):
    return lax.dot_general(a, b, (((1,), (1,)), ((), ())), preferred_element_type=F32)


def dot_nn(a, b):
    return lax.dot_general(a, b, (((1,), (0,)), ((), ())), preferred_element_type=F32)


def main_kernel(
    n,
    pieces,
    lens_ref,
    dest_ref,
    q_hbm,
    do_hbm,
    k_ref,
    v_ref,
    recv,
    tab_v,
    dk_ref,
    dv_ref,
    kv,
    kt,
    vt,
    bias,
    s_scr,
    p_scr,
    ds_scr,
    acc_k,
    acc_v,
    blocks,
    send,
    g_send,
    g_recv,
    kv_ssem,
    kv_rsem,
    g_ssem,
    g_rsem,
    a_ssem,
    a_rsem,
    tab_s,
    tab_sem,
    own_sem,
    q_ref,
    do_ref,
    in_sem,
):
    me = lax.axis_index("ctx")
    tok, width = q_ref.shape
    q_load = pltpu.make_async_copy(q_hbm, q_ref, in_sem.at[0])
    do_load = pltpu.make_async_copy(do_hbm, do_ref, in_sem.at[1])
    heads = width // D
    groups = k_ref.shape[1] // D
    per_group = heads // groups
    chunks = heads // CHUNK
    chunks_group = chunks // groups
    bpd = tok // BLK
    scale = 1.0 / math.sqrt(D)
    log2e_scale = scale * math.log2(math.e)

    barrier = pltpu.get_barrier_semaphore()
    for o in range(1, n):
        pl.semaphore_signal(
            barrier,
            inc=1,
            device_id={"ctx": lax.rem(me + o, n)},
            device_id_type=pl.DeviceIdType.MESH,
        )

    x, y = me // ROW, lax.rem(me, ROW)
    opp = lax.rem(y + ROW // 2, ROW)
    n_rows = n // ROW
    base = ROW - 1
    for g in range(groups):
        kv[base, g, 0] = k_ref[:, g * D : (g + 1) * D]
        kv[base, g, 1] = v_ref[:, g * D : (g + 1) * D]
    pl.semaphore_wait(barrier, n - 1)

    def hop(g, message, src, dst, dx, ty, go):
        @pl.when(go)
        def _():
            pltpu.make_async_remote_copy(
                src_ref=kv.at[base + src, g],
                dst_ref=kv.at[base + dst, g],
                send_sem=kv_ssem.at[message, g],
                recv_sem=kv_rsem.at[base + dst, g],
                device_id={"ctx": (x + dx) * ROW + ty},
                device_id_type=pl.DeviceIdType.MESH,
            ).start()

    def drain(g, message, go):
        @pl.when(go)
        def _():
            held = kv.at[base, g]
            pltpu.make_async_copy(held, held, kv_ssem.at[message, g]).wait()

    def arrive(g, d, go):
        @pl.when(go)
        def _():
            held = kv.at[base + d, g]
            pltpu.make_async_copy(held, held, kv_rsem.at[base + d, g]).wait()

    def beside(k):
        return lax.rem(y + k, ROW)

    below = x < n_rows - 1
    third = (y == ROW - 1) & (x + 3 < n_rows)
    row_go = {k: (beside(k) > y) | (below if k == ROW // 2 else (y < 0)) for k in range(1, ROW)}
    far_opp = (x >= 1) & below & (2 * ROW + y - opp < pieces)
    far_go = {k: (x >= 2) & (2 * ROW + beside(k) - y < pieces) for k in (1, ROW - 1)}

    def stage_one(g):
        hop(g, 0, 0, ROW, 1, y, below)
        for k in (1, 3, 2):
            hop(g, k, 0, beside(k) - y, 0, beside(k), row_go[k])
        hop(g, ROW, 0, 3 * ROW - y, 3, 0, third)

    def stage_two(g):
        arrive(g, ROW, x >= 1)
        hop(g, 5, ROW, 2 * ROW, 1, y, (x >= 1) & below)
        hop(g, 6, ROW, ROW + beside(1) - y, 0, beside(1), x >= 1)
        hop(g, 7, ROW, ROW + beside(ROW - 1) - y, 0, beside(ROW - 1), x >= 1)
        arrive(g, y - opp, below | (y > opp))
        hop(g, 8, y - opp, ROW + y - opp, 1, y, below)

    def stage_three(g):
        arrive(g, 2 * ROW, x >= 2)
        hop(g, 9, 2 * ROW, 2 * ROW + beside(1) - y, 0, beside(1), far_go[1])
        hop(g, 10, 2 * ROW, 2 * ROW + beside(ROW - 1) - y, 0, beside(ROW - 1), far_go[ROW - 1])
        arrive(g, ROW + y - opp, x >= 1)
        hop(g, 11, ROW + y - opp, 2 * ROW + y - opp, 1, y, far_opp)

    def stage_last(g):
        for k in (1, ROW - 1):
            side = beside(k)
            arrive(g, y - side, side < y)
            arrive(g, ROW + y - side, x >= 1)
            arrive(g, 2 * ROW + y - side, (x >= 2) & (2 * ROW + y - side < pieces))
        arrive(g, 2 * ROW + y - opp, (x >= 2) & (2 * ROW + y - opp < pieces))
        arrive(g, 2 * ROW + 1, (x >= 3) & (y == 0))

    def stage_sent(g):
        drain(g, 0, below)
        for k in range(1, ROW):
            drain(g, k, row_go[k])
        drain(g, ROW, third)
        drain(g, 5, (x >= 1) & below)
        drain(g, 6, x >= 1)
        drain(g, 7, x >= 1)
        drain(g, 8, below)
        drain(g, 9, far_go[1])
        drain(g, 10, far_go[ROW - 1])
        drain(g, 11, far_opp)

    def put(g, message, d):
        g_send[message, g, 0] = acc_k[g, d].astype(BF16)
        g_send[message, g, 1] = acc_v[g, d].astype(BF16)

    def ship(g, message, dx, ty):
        pltpu.make_async_remote_copy(
            src_ref=g_send.at[message, g],
            dst_ref=g_recv.at[message, g],
            send_sem=g_ssem.at[message, g],
            recv_sem=g_rsem.at[message, g],
            device_id={"ctx": (x - dx) * ROW + ty},
            device_id_type=pl.DeviceIdType.MESH,
        ).start()

    def give(g, message, d, dx, ty, go):
        @pl.when(go)
        def _():
            put(g, message, d)
            ship(g, message, dx, ty)

    def landed(g, message):
        held = g_recv.at[message, g]
        pltpu.make_async_copy(held, held, g_rsem.at[message, g]).wait()

    def take(g, message, d, go):
        @pl.when(go)
        def _():
            landed(g, message)
            acc_k[g, d] += g_recv[message, g, 0].astype(F32)
            acc_v[g, d] += g_recv[message, g, 1].astype(F32)

    nxt, prv = beside(1), beside(ROW - 1)
    opp_go = below | (opp < y)
    gives = [
        (x >= 2) & (2 * ROW + y - nxt < pieces),
        (x >= 2) & (2 * ROW + y - prv < pieces),
        x >= 1,
        x >= 1,
        (x >= 2) & (2 * ROW + y - opp < pieces),
        nxt < y,
        prv < y,
        (x >= 3) & (y == 0),
        x >= 2,
        x >= 1,
        x >= 1,
        opp_go,
    ]

    def reduce_one(g):
        give(g, 0, 2 * ROW + y - nxt, 0, nxt, gives[0])
        give(g, 1, 2 * ROW + y - prv, 0, prv, gives[1])
        give(g, 4, 2 * ROW + y - opp, 1, y, gives[4])
        give(g, 7, 2 * ROW + 1, 3, ROW - 1, gives[7])
        give(g, 2, ROW + y - nxt, 0, nxt, gives[2])
        give(g, 3, ROW + y - prv, 0, prv, gives[3])
        give(g, 5, y - nxt, 0, nxt, gives[5])
        give(g, 6, y - prv, 0, prv, gives[6])

    def reduce_two(g):
        take(g, 0, 2 * ROW, (x >= 2) & (2 * ROW + prv - y < pieces))
        take(g, 1, 2 * ROW, (x >= 2) & (2 * ROW + nxt - y < pieces))
        give(g, 8, 2 * ROW, 1, y, gives[8])

    def reduce_three(g):
        take(g, 4, ROW + y - opp, (x >= 1) & below & (2 * ROW + y - opp < pieces))
        give(g, 10, ROW + y - opp, 1, y, gives[10])
        take(g, 2, ROW, x >= 1)
        take(g, 3, ROW, x >= 1)
        take(g, 8, ROW, (x >= 1) & below)
        give(g, 9, ROW, 1, y, gives[9])

    def reduce_four(g):
        @pl.when(opp < y)
        def _():
            @pl.when(below)
            def _():
                landed(g, 10)
                acc_k[g, y - opp] += g_recv[10, g, 0].astype(F32)
                acc_v[g, y - opp] += g_recv[10, g, 1].astype(F32)

            put(g, 11, y - opp)

        @pl.when((opp > y) & below)
        def _():
            landed(g, 10)
            g_send[11, g] = g_recv[10, g]

        @pl.when(opp_go)
        def _():
            ship(g, 11, 0, opp)

    def reduce_last(g):
        take(g, 5, 0, y < prv)
        take(g, 6, 0, y < nxt)
        take(g, 7, 0, (y == ROW - 1) & (x + 3 < n_rows))
        take(g, 9, 0, below)
        take(g, 11, 0, below | (y < opp))
        dk_ref[:, g * D : (g + 1) * D] = (acc_k[g, 0] * scale).astype(BF16)
        dv_ref[:, g * D : (g + 1) * D] = acc_v[g, 0].astype(BF16)

    def reduce_sent(g):
        for message, go in enumerate(gives):

            @pl.when(go)
            def _(message=message):
                held = g_send.at[message, g]
                pltpu.make_async_copy(held, held, g_ssem.at[message, g]).wait()

    stage_one(0)
    q_load.start()
    do_load.start()

    for d in range(1, pieces):

        @pl.when(me < d)
        def _(d=d):
            kv[base + d] = jnp.zeros_like(kv[base + d])

    nb = n * bpd
    lane = lax.broadcasted_iota(jnp.int32, (nb, nb), 1)
    sub = lax.broadcasted_iota(jnp.int32, (nb, nb), 0)
    dest_row = jnp.broadcast_to(dest_ref[...], (nb, nb))
    dest_col = dest_row.T
    same = (dest_row // bpd == dest_col // bpd) & (lane // bpd == sub // bpd) & (lane < sub)
    rank = jnp.sum(jnp.where(same, 1.0, 0.0).astype(F32), axis=1, keepdims=True).astype(jnp.int32)
    slot = (dest_col // bpd) * CAP + rank
    picked = (sub // bpd == me) & (slot == lane)
    src_row = jnp.sum(jnp.where(picked, sub - me * bpd, 0), axis=0, keepdims=True)
    tab_v[0:1] = jnp.clip(src_row, 0, bpd - 1)
    found = dest_col == me * bpd + lane
    want_row = jnp.sum(jnp.where(found, (sub // bpd) * CAP + rank, 0), axis=0, keepdims=True)
    tab_v[1:2] = jnp.clip(want_row, 0, n * CAP - 1)
    to_smem = pltpu.make_async_copy(tab_v, tab_s, tab_sem)
    to_smem.start()

    acc_k[...] = jnp.zeros_like(acc_k)
    acc_v[...] = jnp.zeros_like(acc_v)
    query_pos = me * tok + lax.broadcasted_iota(jnp.int32, (1, tok), 1)
    end = jnp.int32(0)
    start = jnp.zeros((1, tok), jnp.int32)
    for doc in range(lens_ref.shape[0]):
        end = end + lens_ref[doc]
        start = start + jnp.where(end <= query_pos, lens_ref[doc], 0)
    for p in range(pieces):
        key_pos = (me - p) * tok + lax.broadcasted_iota(jnp.int32, (tok, tok), 0)
        seen = (key_pos >= start) & (key_pos <= query_pos)
        bias[p] = jnp.where(seen, 0.0, -jnp.inf).astype(F32)

    to_smem.wait()
    stage_two(0)
    stage_three(0)
    q_load.wait()
    do_load.wait()
    for g in range(1, groups):
        stage_one(g)

    def fold(x, op):
        return op(x.reshape(tok // 8, 8, tok), axis=0)

    def pair_step(ch, g):
        cols = [pl.ds(pl.multiple_of((ch * CHUNK + j) * D, D), D) for j in range(CHUNK)]
        qs = [q_ref[:, c] for c in cols]
        dos = [do_ref[:, c] for c in cols]
        peaks, totals = [None] * CHUNK, [None] * CHUNK

        def score(j, p):
            s = dot_nt(kv[base + p, g, 0], qs[j]) + bias[p]
            s_scr[j, p] = s
            top = fold(s, jnp.max)
            peaks[j] = top if p == 0 else jnp.maximum(peaks[j], top)

        def weigh(j, p):
            e = jnp.exp2((s_scr[j, p] - peaks[j]) * log2e_scale)
            s_scr[j, p] = e
            p_scr[j, p * tok : (p + 1) * tok] = e.astype(BF16)
            part = fold(e, jnp.sum)
            totals[j] = part if p == 0 else totals[j] + part

        invs, deltas = [None] * CHUNK, [None] * CHUNK

        def attend(j):
            invs[j] = 1.0 / jnp.sum(totals[j], axis=0, keepdims=True)
            out_t = (dot_nn(vt[g], p_scr[j]) * invs[j]).astype(BF16).astype(F32)
            deltas[j] = jnp.sum(out_t * dos[j].astype(F32).T, axis=0, keepdims=True)
            blocks[0, :, :, j * D : (j + 1) * D] = out_t.T.astype(BF16).reshape(bpd, BLK, D)

        for j in range(CHUNK):
            for p in range(pieces):
                score(j, p)
                if j > 0:
                    weigh(j - 1, p)
            peaks[j] = jnp.max(peaks[j], axis=0, keepdims=True)
            if j > 0:
                attend(j - 1)
        for p in range(pieces):
            weigh(CHUNK - 1, p)
        attend(CHUNK - 1)
        do_cat = jnp.concatenate(dos, axis=0)
        q_cat = jnp.concatenate(qs, axis=0)
        for p in range(pieces):
            pns, dss = [], []
            for j in range(CHUNK):
                dp = dot_nt(kv[base + p, g, 1], dos[j])
                pn = s_scr[j, p] * invs[j]
                ds = (pn * (dp - deltas[j])).astype(BF16)
                ds_scr[j, p * tok : (p + 1) * tok] = ds
                dss.append(ds)
                pns.append(pn.astype(BF16))
            acc_v[g, p] += dot_nn(jnp.concatenate(pns, axis=1), do_cat)
            acc_k[g, p] += dot_nn(jnp.concatenate(dss, axis=1), q_cat)
        for j in range(CHUNK):
            dq_t = dot_nn(kt[g], ds_scr[j]) * scale
            blocks[1, :, :, j * D : (j + 1) * D] = dq_t.T.astype(BF16).reshape(bpd, BLK, D)

    def lanes(ch):
        return pl.ds(pl.multiple_of(ch * CHUNK * D, CHUNK * D), CHUNK * D)

    def block_copy(ch, o):
        target = lax.rem(me + o, n)
        return pltpu.make_async_remote_copy(
            src_ref=send.at[ch, target],
            dst_ref=recv.at[me, :, :, :, lanes(ch)],
            send_sem=a_ssem.at[ch],
            recv_sem=a_rsem.at[ch],
            device_id={"ctx": target},
            device_id_type=pl.DeviceIdType.MESH,
        )

    def own_copy(ch):
        return pltpu.make_async_copy(
            send.at[ch, me], recv.at[me, :, :, :, lanes(ch)], own_sem.at[ch]
        )

    def chunk_step(ch, carry):
        g = ch // chunks_group
        first = lax.rem(ch, chunks_group) == 0
        last = lax.rem(ch, chunks_group) == chunks_group - 1

        @pl.when(first)
        def _():
            stage_last(g)
            for d in range(pieces):
                kt[g, :, d * tok : (d + 1) * tok] = kv[base + d, g, 0].astype(F32).T.astype(BF16)
                vt[g, :, d * tok : (d + 1) * tok] = kv[base + d, g, 1].astype(F32).T.astype(BF16)

        pair_step(ch, g)

        @pl.when(last)
        def _():
            reduce_one(g)

        for t in range(n):
            for c in range(CAP):
                b = tab_s[0, t * CAP + c]
                send[ch, t, c, 0] = blocks[0, b]
                send[ch, t, c, 1] = blocks[1, b]
        for o in range(1, n):
            block_copy(ch, o).start()
        own_copy(ch).start()

        for g2 in range(1, groups):

            @pl.when(ch == (g2 - 1) * chunks_group)
            def _(g2=g2):
                stage_two(g2)

            @pl.when(ch == (g2 - 1) * chunks_group + 1)
            def _(g2=g2):
                stage_three(g2)

            for k, stage in enumerate((reduce_two, reduce_three, reduce_four)):

                @pl.when(ch == g2 * chunks_group + k + 1)
                def _(g2=g2, stage=stage):
                    stage(g2 - 1)

        return carry

    lax.fori_loop(0, chunks, chunk_step, 0)

    reduce_two(groups - 1)
    reduce_three(groups - 1)
    for g in range(groups - 1):
        reduce_last(g)
    reduce_four(groups - 1)
    reduce_last(groups - 1)

    for ch in range(chunks):
        own_copy(ch).wait()
        sent = send.at[ch, pl.ds(0, n - 1)]
        pltpu.make_async_copy(sent, sent, a_ssem.at[ch]).wait()
        held = recv.at[pl.ds(0, n - 1), :, :, :, lanes(ch)]
        pltpu.make_async_copy(held, held, a_rsem.at[ch]).wait()
    for g in range(groups):
        stage_sent(g)
        reduce_sent(g)


def place_kernel(
    tab_ref, recv, dk_in, dv_in, out_ref, dq_ref, dk_ref, dv_ref, held, kept, in_sem, out_sem
):
    bpd = out_ref.shape[0] // BLK
    moves = []
    for slot in range(bpd):
        w = tab_ref[1, slot]
        rows = pl.ds(slot * BLK, BLK)
        for i, ref in enumerate((out_ref, dq_ref)):
            moves.append((recv.at[w // CAP, w % CAP, i], held.at[i, slot], ref.at[rows]))
    for i, (source, ref) in enumerate(((dk_in, dk_ref), (dv_in, dv_ref))):
        moves.append((source, kept.at[i], ref))
    loads = [pltpu.make_async_copy(m[0], m[1], in_sem.at[i]) for i, m in enumerate(moves)]
    stores = [pltpu.make_async_copy(m[1], m[2], out_sem.at[i]) for i, m in enumerate(moves)]
    for load in loads:
        load.start()
    for load, store in zip(loads, stores):
        load.wait()
        store.start()
    for store in stores:
        store.wait()


def shards(q, k, v, do, lens, dest):
    n = lax.axis_size("ctx")
    tok, width = q.shape
    heads = width // D
    groups = k.shape[1] // D
    bpd = tok // BLK
    pieces = min(n, (MAX_DOC - 1 + tok - 1) // tok + 1)
    chunks = heads // CHUNK
    keys = pieces * tok
    smem = pl.BlockSpec(memory_space=pltpu.SMEM)
    vmem = pl.BlockSpec(memory_space=pltpu.VMEM)
    hbm = pl.BlockSpec(memory_space=pl.ANY)
    recv, tab, dk, dv = pl.pallas_call(
        functools.partial(main_kernel, n, pieces),
        out_shape=(
            jax.ShapeDtypeStruct((n, CAP, 2, BLK, width), BF16),
            jax.ShapeDtypeStruct((2, n * bpd), jnp.int32),
            jax.ShapeDtypeStruct(k.shape, BF16),
            jax.ShapeDtypeStruct(v.shape, BF16),
        ),
        in_specs=[smem, vmem, hbm, hbm, vmem, vmem],
        out_specs=(hbm, vmem, vmem, vmem),
        scratch_shapes=[
            pltpu.VMEM((4 * ROW - 1, groups, 2, tok, D), BF16),
            pltpu.VMEM((groups, D, keys), BF16),
            pltpu.VMEM((groups, D, keys), BF16),
            pltpu.VMEM((pieces, tok, tok), F32),
            pltpu.VMEM((CHUNK, pieces, tok, tok), F32),
            pltpu.VMEM((CHUNK, keys, tok), BF16),
            pltpu.VMEM((CHUNK, keys, tok), BF16),
            pltpu.VMEM((groups, pieces, tok, D), F32),
            pltpu.VMEM((groups, pieces, tok, D), F32),
            pltpu.VMEM((2, bpd, BLK, CHUNK * D), BF16),
            pltpu.VMEM((chunks, n, CAP, 2, BLK, CHUNK * D), BF16),
            pltpu.VMEM((3 * ROW, groups, 2, tok, D), BF16),
            pltpu.VMEM((3 * ROW, groups, 2, tok, D), BF16),
            pltpu.SemaphoreType.DMA((3 * ROW, groups)),
            pltpu.SemaphoreType.DMA((4 * ROW - 1, groups)),
            pltpu.SemaphoreType.DMA((3 * ROW, groups)),
            pltpu.SemaphoreType.DMA((3 * ROW, groups)),
            pltpu.SemaphoreType.DMA((chunks,)),
            pltpu.SemaphoreType.DMA((chunks,)),
            pltpu.SMEM((2, n * bpd), jnp.int32),
            pltpu.SemaphoreType.DMA(()),
            pltpu.SemaphoreType.DMA((chunks,)),
            pltpu.VMEM(q.shape, BF16),
            pltpu.VMEM(q.shape, BF16),
            pltpu.SemaphoreType.DMA((2,)),
        ],
        compiler_params=pltpu.CompilerParams(
            collective_id=0, has_side_effects=True, vmem_limit_bytes=60 * 2**20
        ),
    )(lens, dest.reshape(1, n * bpd), q, do, k, v)
    return pl.pallas_call(
        place_kernel,
        out_shape=(
            jax.ShapeDtypeStruct(q.shape, BF16),
            jax.ShapeDtypeStruct(q.shape, BF16),
            jax.ShapeDtypeStruct(k.shape, BF16),
            jax.ShapeDtypeStruct(v.shape, BF16),
        ),
        in_specs=[smem, hbm, hbm, hbm],
        out_specs=(hbm, hbm, hbm, hbm),
        scratch_shapes=[
            pltpu.VMEM((2, bpd, BLK, width), BF16),
            pltpu.VMEM((2, *k.shape), BF16),
            pltpu.SemaphoreType.DMA((2 * bpd + 2,)),
            pltpu.SemaphoreType.DMA((2 * bpd + 2,)),
        ],
    )(tab, recv, dk, dv)


def solution(mesh):
    rows = P(("dp", "ctx"), "head")
    return jax.shard_map(
        shards,
        mesh=mesh,
        in_specs=(rows, rows, rows, rows, P("dp"), P("dp")),
        out_specs=(rows, rows, rows, rows),
        check_vma=False,
    )
```

```python
import functools
import math

import jax
import jax.numpy as jnp
from jax import lax
from jax.experimental import pallas as pl
from jax.experimental.pallas import tpu as pltpu
from jax.sharding import PartitionSpec as P

D = 128
BLK = 16
MAX_DOC = 2304
CAP = 2
CHUNK = 2
ROW = 4
F32 = jnp.float32
BF16 = jnp.bfloat16


def dot_nt(a, b):
    return lax.dot_general(a, b, (((1,), (1,)), ((), ())), preferred_element_type=F32)


def dot_nn(a, b):
    return lax.dot_general(a, b, (((1,), (0,)), ((), ())), preferred_element_type=F32)


def main_kernel(
    n,
    pieces,
    lens_ref,
    dest_ref,
    q_hbm,
    do_hbm,
    k_ref,
    v_ref,
    recv,
    tab_v,
    dk_ref,
    dv_ref,
    kv,
    kt,
    vt,
    bias,
    s_scr,
    p_scr,
    ds_scr,
    acc_k,
    acc_v,
    blocks,
    send,
    g_send,
    g_recv,
    kv_ssem,
    kv_rsem,
    g_ssem,
    g_rsem,
    a_ssem,
    a_rsem,
    tab_s,
    tab_sem,
    own_sem,
    q_ref,
    do_ref,
    in_sem,
):
    me = lax.axis_index("ctx")
    tok, width = q_ref.shape
    q_load = pltpu.make_async_copy(q_hbm, q_ref, in_sem.at[0])
    do_load = pltpu.make_async_copy(do_hbm, do_ref, in_sem.at[1])
    heads = width // D
    groups = k_ref.shape[1] // D
    per_group = heads // groups
    chunks = heads // CHUNK
    chunks_group = chunks // groups
    bpd = tok // BLK
    scale = 1.0 / math.sqrt(D)
    log2e_scale = scale * math.log2(math.e)

    barrier = pltpu.get_barrier_semaphore()
    for o in range(1, n):
        pl.semaphore_signal(
            barrier,
            inc=1,
            device_id={"ctx": lax.rem(me + o, n)},
            device_id_type=pl.DeviceIdType.MESH,
        )

    x, y = me // ROW, lax.rem(me, ROW)
    opp = lax.rem(y + ROW // 2, ROW)
    n_rows = n // ROW
    base = ROW - 1
    for g in range(groups):
        kv[base, g, 0] = k_ref[:, g * D : (g + 1) * D]
        kv[base, g, 1] = v_ref[:, g * D : (g + 1) * D]
    pl.semaphore_wait(barrier, n - 1)

    def hop(g, message, src, dst, dx, ty, go):
        @pl.when(go)
        def _():
            pltpu.make_async_remote_copy(
                src_ref=kv.at[base + src, g],
                dst_ref=kv.at[base + dst, g],
                send_sem=kv_ssem.at[message, g],
                recv_sem=kv_rsem.at[base + dst, g],
                device_id={"ctx": (x + dx) * ROW + ty},
                device_id_type=pl.DeviceIdType.MESH,
            ).start()

    def drain(g, message, go):
        @pl.when(go)
        def _():
            held = kv.at[base, g]
            pltpu.make_async_copy(held, held, kv_ssem.at[message, g]).wait()

    def arrive(g, d, go):
        @pl.when(go)
        def _():
            held = kv.at[base + d, g]
            pltpu.make_async_copy(held, held, kv_rsem.at[base + d, g]).wait()

    def beside(k):
        return lax.rem(y + k, ROW)

    below = x < n_rows - 1
    third = (y == ROW - 1) & (x + 3 < n_rows)
    row_go = {k: (beside(k) > y) | (below if k == ROW // 2 else (y < 0)) for k in range(1, ROW)}
    far_opp = (x >= 1) & below & (2 * ROW + y - opp < pieces)
    far_go = {k: (x >= 2) & (2 * ROW + beside(k) - y < pieces) for k in (1, ROW - 1)}

    def stage_one(g):
        hop(g, 0, 0, ROW, 1, y, below)
        for k in (1, 3, 2):
            hop(g, k, 0, beside(k) - y, 0, beside(k), row_go[k])
        hop(g, ROW, 0, 3 * ROW - y, 3, 0, third)

    def stage_two(g):
        arrive(g, ROW, x >= 1)
        hop(g, 5, ROW, 2 * ROW, 1, y, (x >= 1) & below)
        hop(g, 6, ROW, ROW + beside(1) - y, 0, beside(1), x >= 1)
        hop(g, 7, ROW, ROW + beside(ROW - 1) - y, 0, beside(ROW - 1), x >= 1)
        arrive(g, y - opp, below | (y > opp))
        hop(g, 8, y - opp, ROW + y - opp, 1, y, below)

    def stage_three(g):
        arrive(g, 2 * ROW, x >= 2)
        hop(g, 9, 2 * ROW, 2 * ROW + beside(1) - y, 0, beside(1), far_go[1])
        hop(g, 10, 2 * ROW, 2 * ROW + beside(ROW - 1) - y, 0, beside(ROW - 1), far_go[ROW - 1])
        arrive(g, ROW + y - opp, x >= 1)
        hop(g, 11, ROW + y - opp, 2 * ROW + y - opp, 1, y, far_opp)

    def stage_last(g):
        for k in (1, ROW - 1):
            side = beside(k)
            arrive(g, y - side, side < y)
            arrive(g, ROW + y - side, x >= 1)
            arrive(g, 2 * ROW + y - side, (x >= 2) & (2 * ROW + y - side < pieces))
        arrive(g, 2 * ROW + y - opp, (x >= 2) & (2 * ROW + y - opp < pieces))
        arrive(g, 2 * ROW + 1, (x >= 3) & (y == 0))

    def stage_sent(g):
        drain(g, 0, below)
        for k in range(1, ROW):
            drain(g, k, row_go[k])
        drain(g, ROW, third)
        drain(g, 5, (x >= 1) & below)
        drain(g, 6, x >= 1)
        drain(g, 7, x >= 1)
        drain(g, 8, below)
        drain(g, 9, far_go[1])
        drain(g, 10, far_go[ROW - 1])
        drain(g, 11, far_opp)

    def put(g, message, d):
        g_send[message, g, 0] = acc_k[g, d].astype(BF16)
        g_send[message, g, 1] = acc_v[g, d].astype(BF16)

    def ship(g, message, dx, ty):
        pltpu.make_async_remote_copy(
            src_ref=g_send.at[message, g],
            dst_ref=g_recv.at[message, g],
            send_sem=g_ssem.at[message, g],
            recv_sem=g_rsem.at[message, g],
            device_id={"ctx": (x - dx) * ROW + ty},
            device_id_type=pl.DeviceIdType.MESH,
        ).start()

    def give(g, message, d, dx, ty, go):
        @pl.when(go)
        def _():
            put(g, message, d)
            ship(g, message, dx, ty)

    def landed(g, message):
        held = g_recv.at[message, g]
        pltpu.make_async_copy(held, held, g_rsem.at[message, g]).wait()

    def take(g, message, d, go):
        @pl.when(go)
        def _():
            landed(g, message)
            acc_k[g, d] += g_recv[message, g, 0].astype(F32)
            acc_v[g, d] += g_recv[message, g, 1].astype(F32)

    nxt, prv = beside(1), beside(ROW - 1)
    opp_go = below | (opp < y)
    gives = [
        (x >= 2) & (2 * ROW + y - nxt < pieces),
        (x >= 2) & (2 * ROW + y - prv < pieces),
        x >= 1,
        x >= 1,
        (x >= 2) & (2 * ROW + y - opp < pieces),
        nxt < y,
        prv < y,
        (x >= 3) & (y == 0),
        x >= 2,
        x >= 1,
        x >= 1,
        opp_go,
    ]

    def reduce_one(g):
        give(g, 4, 2 * ROW + y - opp, 1, y, gives[4])
        give(g, 0, 2 * ROW + y - nxt, 0, nxt, gives[0])
        give(g, 1, 2 * ROW + y - prv, 0, prv, gives[1])
        give(g, 7, 2 * ROW + 1, 3, ROW - 1, gives[7])
        give(g, 2, ROW + y - nxt, 0, nxt, gives[2])
        give(g, 3, ROW + y - prv, 0, prv, gives[3])
        give(g, 5, y - nxt, 0, nxt, gives[5])
        give(g, 6, y - prv, 0, prv, gives[6])

    def reduce_two(g):
        take(g, 0, 2 * ROW, (x >= 2) & (2 * ROW + prv - y < pieces))
        take(g, 1, 2 * ROW, (x >= 2) & (2 * ROW + nxt - y < pieces))
        give(g, 8, 2 * ROW, 1, y, gives[8])
        take(g, 4, ROW + y - opp, (x >= 1) & below & (2 * ROW + y - opp < pieces))
        give(g, 10, ROW + y - opp, 1, y, gives[10])

    def reduce_three(g):
        take(g, 2, ROW, x >= 1)
        take(g, 3, ROW, x >= 1)
        take(g, 8, ROW, (x >= 1) & below)
        give(g, 9, ROW, 1, y, gives[9])

    def reduce_four(g):
        @pl.when(opp < y)
        def _():
            @pl.when(below)
            def _():
                landed(g, 10)
                acc_k[g, y - opp] += g_recv[10, g, 0].astype(F32)
                acc_v[g, y - opp] += g_recv[10, g, 1].astype(F32)

            put(g, 11, y - opp)

        @pl.when((opp > y) & below)
        def _():
            landed(g, 10)
            g_send[11, g] = g_recv[10, g]

        @pl.when(opp_go)
        def _():
            ship(g, 11, 0, opp)

    def reduce_last(g):
        take(g, 5, 0, y < prv)
        take(g, 6, 0, y < nxt)
        take(g, 7, 0, (y == ROW - 1) & (x + 3 < n_rows))
        take(g, 9, 0, below)
        take(g, 11, 0, below | (y < opp))
        dk_ref[:, g * D : (g + 1) * D] = (acc_k[g, 0] * scale).astype(BF16)
        dv_ref[:, g * D : (g + 1) * D] = acc_v[g, 0].astype(BF16)

    def reduce_sent(g):
        for message, go in enumerate(gives):

            @pl.when(go)
            def _(message=message):
                held = g_send.at[message, g]
                pltpu.make_async_copy(held, held, g_ssem.at[message, g]).wait()

    stage_one(0)
    q_load.start()
    do_load.start()

    for d in range(1, pieces):

        @pl.when(me < d)
        def _(d=d):
            kv[base + d] = jnp.zeros_like(kv[base + d])

    nb = n * bpd
    lane = lax.broadcasted_iota(jnp.int32, (nb, nb), 1)
    sub = lax.broadcasted_iota(jnp.int32, (nb, nb), 0)
    dest_row = jnp.broadcast_to(dest_ref[...], (nb, nb))
    dest_col = dest_row.T
    same = (dest_row // bpd == dest_col // bpd) & (lane // bpd == sub // bpd) & (lane < sub)
    rank = jnp.sum(jnp.where(same, 1.0, 0.0).astype(F32), axis=1, keepdims=True).astype(jnp.int32)
    slot = (dest_col // bpd) * CAP + rank
    picked = (sub // bpd == me) & (slot == lane)
    src_row = jnp.sum(jnp.where(picked, sub - me * bpd, 0), axis=0, keepdims=True)
    tab_v[0:1] = jnp.clip(src_row, 0, bpd - 1)
    found = dest_col == me * bpd + lane
    want_row = jnp.sum(jnp.where(found, (sub // bpd) * CAP + rank, 0), axis=0, keepdims=True)
    tab_v[1:2] = jnp.clip(want_row, 0, n * CAP - 1)
    to_smem = pltpu.make_async_copy(tab_v, tab_s, tab_sem)
    to_smem.start()

    acc_k[...] = jnp.zeros_like(acc_k)
    acc_v[...] = jnp.zeros_like(acc_v)
    query_pos = me * tok + lax.broadcasted_iota(jnp.int32, (1, tok), 1)
    end = jnp.int32(0)
    start = jnp.zeros((1, tok), jnp.int32)
    for doc in range(lens_ref.shape[0]):
        end = end + lens_ref[doc]
        start = start + jnp.where(end <= query_pos, lens_ref[doc], 0)
    for p in range(pieces):
        key_pos = (me - p) * tok + lax.broadcasted_iota(jnp.int32, (tok, tok), 0)
        seen = (key_pos >= start) & (key_pos <= query_pos)
        bias[p] = jnp.where(seen, 0.0, -jnp.inf).astype(F32)

    to_smem.wait()
    stage_two(0)
    stage_three(0)
    q_load.wait()
    do_load.wait()
    for g in range(1, groups):
        stage_one(g)

    def fold(x, op):
        return op(x.reshape(tok // 8, 8, tok), axis=0)

    def pair_step(ch, g):
        cols = [pl.ds(pl.multiple_of((ch * CHUNK + j) * D, D), D) for j in range(CHUNK)]
        qs = [q_ref[:, c] for c in cols]
        dos = [do_ref[:, c] for c in cols]
        peaks, totals = [None] * CHUNK, [None] * CHUNK

        def score(j, p):
            s = dot_nt(kv[base + p, g, 0], qs[j]) + bias[p]
            s_scr[j, p] = s
            top = fold(s, jnp.max)
            peaks[j] = top if p == 0 else jnp.maximum(peaks[j], top)

        def weigh(j, p):
            e = jnp.exp2((s_scr[j, p] - peaks[j]) * log2e_scale)
            s_scr[j, p] = e
            p_scr[j, p * tok : (p + 1) * tok] = e.astype(BF16)
            part = fold(e, jnp.sum)
            totals[j] = part if p == 0 else totals[j] + part

        invs, deltas = [None] * CHUNK, [None] * CHUNK

        def attend(j):
            invs[j] = 1.0 / jnp.sum(totals[j], axis=0, keepdims=True)
            out_t = (dot_nn(vt[g], p_scr[j]) * invs[j]).astype(BF16).astype(F32)
            deltas[j] = jnp.sum(out_t * dos[j].astype(F32).T, axis=0, keepdims=True)
            blocks[0, :, :, j * D : (j + 1) * D] = out_t.T.astype(BF16).reshape(bpd, BLK, D)

        for j in range(CHUNK):
            for p in range(pieces):
                score(j, p)
                if j > 0:
                    weigh(j - 1, p)
            peaks[j] = jnp.max(peaks[j], axis=0, keepdims=True)
            if j > 0:
                attend(j - 1)
        for p in range(pieces):
            weigh(CHUNK - 1, p)
        attend(CHUNK - 1)
        do_cat = jnp.concatenate(dos, axis=0)
        q_cat = jnp.concatenate(qs, axis=0)
        for p in range(pieces):
            pns, dss = [], []
            for j in range(CHUNK):
                dp = dot_nt(kv[base + p, g, 1], dos[j])
                pn = s_scr[j, p] * invs[j]
                ds = (pn * (dp - deltas[j])).astype(BF16)
                ds_scr[j, p * tok : (p + 1) * tok] = ds
                dss.append(ds)
                pns.append(pn.astype(BF16))
            acc_v[g, p] += dot_nn(jnp.concatenate(pns, axis=1), do_cat)
            acc_k[g, p] += dot_nn(jnp.concatenate(dss, axis=1), q_cat)
        for j in range(CHUNK):
            dq_t = dot_nn(kt[g], ds_scr[j]) * scale
            blocks[1, :, :, j * D : (j + 1) * D] = dq_t.T.astype(BF16).reshape(bpd, BLK, D)

    def lanes(ch):
        return pl.ds(pl.multiple_of(ch * CHUNK * D, CHUNK * D), CHUNK * D)

    def block_copy(ch, o):
        target = lax.rem(me + o, n)
        return pltpu.make_async_remote_copy(
            src_ref=send.at[ch, target],
            dst_ref=recv.at[me, :, :, :, lanes(ch)],
            send_sem=a_ssem.at[ch],
            recv_sem=a_rsem.at[ch],
            device_id={"ctx": target},
            device_id_type=pl.DeviceIdType.MESH,
        )

    def own_copy(ch):
        return pltpu.make_async_copy(
            send.at[ch, me], recv.at[me, :, :, :, lanes(ch)], own_sem.at[ch]
        )

    def chunk_step(ch, carry):
        g = ch // chunks_group
        first = lax.rem(ch, chunks_group) == 0
        last = lax.rem(ch, chunks_group) == chunks_group - 1

        @pl.when(first)
        def _():
            stage_last(g)
            for d in range(pieces):
                kt[g, :, d * tok : (d + 1) * tok] = kv[base + d, g, 0].astype(F32).T.astype(BF16)
                vt[g, :, d * tok : (d + 1) * tok] = kv[base + d, g, 1].astype(F32).T.astype(BF16)

        pair_step(ch, g)

        @pl.when(last)
        def _():
            reduce_one(g)

        for t in range(n):
            for c in range(CAP):
                b = tab_s[0, t * CAP + c]
                send[ch, t, c, 0] = blocks[0, b]
                send[ch, t, c, 1] = blocks[1, b]
        held_back = chunks - 2

        @pl.when(ch == held_back + 1)
        def _():
            for o in range(1, n):
                block_copy(ch - 1, o).start()
            own_copy(ch - 1).start()

        @pl.when(ch != held_back)
        def _():
            for o in range(1, n):
                block_copy(ch, o).start()
            own_copy(ch).start()

        for g2 in range(1, groups):

            @pl.when(ch == (g2 - 1) * chunks_group)
            def _(g2=g2):
                stage_two(g2)

            @pl.when(ch == (g2 - 1) * chunks_group + 1)
            def _(g2=g2):
                stage_three(g2)

            for k, stage in enumerate((reduce_two, reduce_three, reduce_four)):

                @pl.when(ch == g2 * chunks_group + k + 1)
                def _(g2=g2, stage=stage):
                    stage(g2 - 1)

        return carry

    lax.fori_loop(0, chunks, chunk_step, 0)

    reduce_two(groups - 1)
    reduce_three(groups - 1)
    for g in range(groups - 1):
        reduce_last(g)
    reduce_four(groups - 1)
    reduce_last(groups - 1)

    for ch in range(chunks):
        own_copy(ch).wait()
        sent = send.at[ch, pl.ds(0, n - 1)]
        pltpu.make_async_copy(sent, sent, a_ssem.at[ch]).wait()
        held = recv.at[pl.ds(0, n - 1), :, :, :, lanes(ch)]
        pltpu.make_async_copy(held, held, a_rsem.at[ch]).wait()
    for g in range(groups):
        stage_sent(g)
        reduce_sent(g)


def place_kernel(
    tab_ref, recv, dk_in, dv_in, out_ref, dq_ref, dk_ref, dv_ref, held, kept, in_sem, out_sem
):
    bpd = out_ref.shape[0] // BLK
    loads, stores = [], []
    for slot in range(bpd):
        w = tab_ref[1, slot]
        rows = pl.ds(slot * BLK, BLK)
        loads.append(
            pltpu.make_async_copy(recv.at[w // CAP, w % CAP], held.at[slot], in_sem.at[slot])
        )
        stores.append(
            [
                pltpu.make_async_copy(held.at[slot, i], ref.at[rows], out_sem.at[2 * slot + i])
                for i, ref in enumerate((out_ref, dq_ref))
            ]
        )
    for i, (source, ref) in enumerate(((dk_in, dk_ref), (dv_in, dv_ref))):
        loads.append(pltpu.make_async_copy(source, kept.at[i], in_sem.at[bpd + i]))
        stores.append([pltpu.make_async_copy(kept.at[i], ref, out_sem.at[2 * bpd + i])])
    for load in loads:
        load.start()
    for load, group in zip(loads, stores):
        load.wait()
        for store in group:
            store.start()
    for group in stores:
        for store in group:
            store.wait()


def shards(q, k, v, do, lens, dest):
    n = lax.axis_size("ctx")
    tok, width = q.shape
    heads = width // D
    groups = k.shape[1] // D
    bpd = tok // BLK
    pieces = min(n, (MAX_DOC - 1 + tok - 1) // tok + 1)
    chunks = heads // CHUNK
    keys = pieces * tok
    smem = pl.BlockSpec(memory_space=pltpu.SMEM)
    vmem = pl.BlockSpec(memory_space=pltpu.VMEM)
    hbm = pl.BlockSpec(memory_space=pl.ANY)
    recv, tab, dk, dv = pl.pallas_call(
        functools.partial(main_kernel, n, pieces),
        out_shape=(
            jax.ShapeDtypeStruct((n, CAP, 2, BLK, width), BF16),
            jax.ShapeDtypeStruct((2, n * bpd), jnp.int32),
            jax.ShapeDtypeStruct(k.shape, BF16),
            jax.ShapeDtypeStruct(v.shape, BF16),
        ),
        in_specs=[smem, vmem, hbm, hbm, vmem, vmem],
        out_specs=(hbm, vmem, vmem, vmem),
        scratch_shapes=[
            pltpu.VMEM((4 * ROW - 1, groups, 2, tok, D), BF16),
            pltpu.VMEM((groups, D, keys), BF16),
            pltpu.VMEM((groups, D, keys), BF16),
            pltpu.VMEM((pieces, tok, tok), F32),
            pltpu.VMEM((CHUNK, pieces, tok, tok), F32),
            pltpu.VMEM((CHUNK, keys, tok), BF16),
            pltpu.VMEM((CHUNK, keys, tok), BF16),
            pltpu.VMEM((groups, pieces, tok, D), F32),
            pltpu.VMEM((groups, pieces, tok, D), F32),
            pltpu.VMEM((2, bpd, BLK, CHUNK * D), BF16),
            pltpu.VMEM((chunks, n, CAP, 2, BLK, CHUNK * D), BF16),
            pltpu.VMEM((3 * ROW, groups, 2, tok, D), BF16),
            pltpu.VMEM((3 * ROW, groups, 2, tok, D), BF16),
            pltpu.SemaphoreType.DMA((3 * ROW, groups)),
            pltpu.SemaphoreType.DMA((4 * ROW - 1, groups)),
            pltpu.SemaphoreType.DMA((3 * ROW, groups)),
            pltpu.SemaphoreType.DMA((3 * ROW, groups)),
            pltpu.SemaphoreType.DMA((chunks,)),
            pltpu.SemaphoreType.DMA((chunks,)),
            pltpu.SMEM((2, n * bpd), jnp.int32),
            pltpu.SemaphoreType.DMA(()),
            pltpu.SemaphoreType.DMA((chunks,)),
            pltpu.VMEM(q.shape, BF16),
            pltpu.VMEM(q.shape, BF16),
            pltpu.SemaphoreType.DMA((2,)),
        ],
        compiler_params=pltpu.CompilerParams(
            collective_id=0, has_side_effects=True, vmem_limit_bytes=60 * 2**20
        ),
    )(lens, dest.reshape(1, n * bpd), q, do, k, v)
    return pl.pallas_call(
        place_kernel,
        out_shape=(
            jax.ShapeDtypeStruct(q.shape, BF16),
            jax.ShapeDtypeStruct(q.shape, BF16),
            jax.ShapeDtypeStruct(k.shape, BF16),
            jax.ShapeDtypeStruct(v.shape, BF16),
        ),
        in_specs=[smem, hbm, hbm, hbm],
        out_specs=(hbm, hbm, hbm, hbm),
        scratch_shapes=[
            pltpu.VMEM((bpd, 2, BLK, width), BF16),
            pltpu.VMEM((2, *k.shape), BF16),
            pltpu.SemaphoreType.DMA((bpd + 2,)),
            pltpu.SemaphoreType.DMA((2 * bpd + 2,)),
        ],
    )(tab, recv, dk, dv)


def solution(mesh):
    rows = P(("dp", "ctx"), "head")
    return jax.shard_map(
        shards,
        mesh=mesh,
        in_specs=(rows, rows, rows, rows, P("dp"), P("dp")),
        out_specs=(rows, rows, rows, rows),
        check_vma=False,
    )
```
